32 devices in a mesh: patch: 2 (over y), epoch: 4 (over z), tile: 4 (over x, core).
Axes of the slice: x: 2, y: 2, z: 4, core: 2. Of those that a mesh axis runs over, the one named last changes fastest.
Arguments:
- template: float32 [768, 512], P(('patch', 'epoch'), 'tile'), parts along dimension 0, may hold values from -14.2 to 14.2
- science: float32 [8, 384, 512], P(('patch', 'epoch'), None, 'tile'), parts along dimension 0, may hold values from -31 to 31
- row_profiles: float32 [12, 21], replicated, may hold values from -1.25 to 1.25
- col_profiles: float32 [12, 21], replicated, may hold values from -1.25 to 1.25
- coverage: int32 [8, 256], P(('patch', 'epoch'), 'tile'), parts along dimension 0, may hold values 0 or 1
- stamp_rows: int32 [512], P(('patch', 'tile')), parts along dimension 0, may hold values from 0 to 352
- stamp_cols: int32 [512], P(('patch', 'tile')), parts along dimension 0, may hold values from 0 to 96
Outputs:
- difference: float32 [8, 384, 512], P(('patch', 'epoch'), None, 'tile'), parts along dimension 0
The draws below stay inside these ranges and needn't reach their ends.
There are 2 independent parts, one for each index of `patch`. The reference program is written for one: setup_inputs(seed, part) draws one part's arguments, and reference() takes and returns one part's arrays. A program takes and returns all parts, laid end to end along the dimension named above; an argument that names none is the same for every part. Nothing has to cross between parts.
All inputs are finite; a program needn't handle non-finite values. No bound on the sum of `coverage` on one device may be relied on, other than what follows from the above.
Results may differ from the reference program's by a relative error of at most 0.00011.
Values sent between devices are 32-bit elements; how exact they have to be, the bound alone decides.
A program may use at most 128 MiB of HBM per device.

```python
import jax
import jax.numpy as jnp
from jax import lax

NB = 12
KER = 21
S = 32
NS_TILE = 64
NR = 384
CW = 128
NC = 512
VISITS = 4
NSTAMP = 256


def patch_base(key):
    field = jax.random.normal(jax.random.fold_in(key, 11), (NR, NC), jnp.float32)
    field = jnp.clip(field, -5.0, 5.0)
    return field


def draw_template(key, part):
    return patch_base(key)


def draw_science(key, part):
    field = patch_base(key)
    gains = jnp.exp(jax.random.uniform(jax.random.fold_in(key, 12), (VISITS, 1, 1), jnp.float32, -0.7, 0.7))
    noise = jnp.clip(jax.random.normal(jax.random.fold_in(key, 14), (VISITS, NR, NC), jnp.float32), -5.0, 5.0)
    blended = 0.6 * field + 0.4 * jnp.roll(field, 1, axis=1)
    return gains * blended[None] + 0.3 * noise


def with_ends(drawn, rng, smallest, largest):
    spot = [jax.random.randint(jax.random.fold_in(rng, axis), (), 0, length) for axis, length in enumerate(drawn.shape)]
    longest = drawn.shape.index(max(drawn.shape))
    next_to = spot[:longest] + [(spot[longest] + 1) % drawn.shape[longest]] + spot[longest + 1:]
    return drawn.at[tuple(spot)].set(smallest).at[tuple(next_to)].set(largest)


def bell_draw(key, dims, width, reach, kind=jnp.bfloat16):
    values = jax.random.normal(key, dims, jnp.float32) * width
    return jnp.minimum(jnp.maximum(values, -reach), reach).astype(kind)


def setup_inputs(seed: int = 0, part: int = 0) -> dict:
    seeds = jax.random.split(jax.random.key(seed), 8)
    part_keys = jax.random.split(jax.random.fold_in(seeds[7], part), 8)
    template = draw_template(jax.random.fold_in(jax.random.fold_in(seeds[7], part), 71), part)
    science = draw_science(jax.random.fold_in(jax.random.fold_in(seeds[7], part), 71), part)
    row_profiles = bell_draw(seeds[2], (NB, KER), KER ** -0.5, 1.25, jnp.float32)
    col_profiles = bell_draw(seeds[3], (NB, KER), KER ** -0.5, 1.25, jnp.float32)
    coverage = with_ends((jax.random.randint(part_keys[4], (VISITS, NSTAMP), 0, 4) < 3).astype(jnp.int32), jax.random.fold_in(part_keys[4], 1), 0, 1)
    stamp_rows = with_ends(jax.random.randint(part_keys[5], (NSTAMP,), 0, NR - S + 1), jax.random.fold_in(part_keys[5], 1), 0, NR - S).astype(jnp.int32)
    stamp_cols = with_ends(jax.random.randint(part_keys[6], (NSTAMP,), 0, CW - S + 1), jax.random.fold_in(part_keys[6], 1), 0, CW - S).astype(jnp.int32)
    return dict(template=template, science=science, row_profiles=row_profiles, col_profiles=col_profiles, coverage=coverage, stamp_rows=stamp_rows, stamp_cols=stamp_cols)


ridge_weight = 1.0

def build_features(windows, xi_win, eta_win):
    count = windows.shape[0]
    stacked = jnp.stack([windows, windows * xi_win[:, None, None, :], windows * eta_win[:, None, :, None]], axis=2)
    flattened = stacked.reshape(count, 3 * NB, S * S)
    constant = jnp.ones((count, 1, S * S), jnp.float32)
    return jnp.concatenate([flattened, constant], axis=1)

def reference(template, science, row_profiles, col_profiles, coverage, stamp_rows, stamp_cols):
    half_width = KER // 2
    padded = jnp.pad(template, half_width)
    across = jnp.zeros((NB, NR + 2 * half_width, NC), jnp.float32)
    for offset in range(KER):
        across = across + col_profiles[:, offset][:, None, None] * padded[None, :, offset:offset + NC]
    images = jnp.zeros((NB, NR, NC), jnp.float32)
    for offset in range(KER):
        images = images + row_profiles[:, offset][:, None, None] * across[:, offset:offset + NR, :]
    strip_of = (jnp.arange(NSTAMP) // NS_TILE).astype(jnp.int32)
    global_cols = (strip_of * CW + stamp_cols).astype(jnp.int32)
    zero_index = jnp.zeros((), jnp.int32)
    xi_all = 2.0 * jnp.arange(NC).astype(jnp.float32) / NC - 1.0
    eta_all = 2.0 * jnp.arange(NR).astype(jnp.float32) / NR - 1.0

    def cut_stamp(row_at, col_at):
        return lax.dynamic_slice(images, (zero_index, row_at, col_at), (NB, S, S))
    windows = jax.vmap(cut_stamp)(stamp_rows, global_cols)
    xi_win = jax.vmap(lambda col_at: lax.dynamic_slice_in_dim(xi_all, col_at, S))(global_cols)
    eta_win = jax.vmap(lambda row_at: lax.dynamic_slice_in_dim(eta_all, row_at, S))(stamp_rows)
    features = build_features(windows, xi_win, eta_win)
    stamp_grams = jnp.einsum('sfp,sgp->sfg', features, features, precision=lax.Precision.HIGHEST)
    weights = coverage.astype(jnp.float32)
    grams = jnp.einsum('vs,sfg->vfg', weights, stamp_grams, precision=lax.Precision.HIGHEST)
    unknowns = 3 * NB + 1

    def per_visit(items):
        visit_image, visit_weights, normal_matrix = items
        sci_win = jax.vmap(lambda row_at, col_at: lax.dynamic_slice(visit_image, (row_at, col_at), (S, S)))(stamp_rows, global_cols)
        weighted = features * visit_weights[:, None, None]
        normal_rhs = jnp.einsum('sfp,sp->f', weighted, sci_win.reshape(NSTAMP, S * S), precision=lax.Precision.HIGHEST)
        system = normal_matrix + ridge_weight * jnp.eye(unknowns, dtype=jnp.float32)
        factor = jnp.linalg.cholesky(system)
        coefficients = jax.scipy.linalg.cho_solve((factor, True), normal_rhs)
        per_basis = coefficients[:3 * NB].reshape(NB, 3)
        model_field = jnp.einsum('b,byx->yx', per_basis[:, 0], images, precision=lax.Precision.HIGHEST)
        model_field = model_field + xi_all[None, :] * jnp.einsum('b,byx->yx', per_basis[:, 1], images, precision=lax.Precision.HIGHEST)
        model_field = model_field + eta_all[:, None] * jnp.einsum('b,byx->yx', per_basis[:, 2], images, precision=lax.Precision.HIGHEST)
        model_field = model_field + coefficients[3 * NB]
        return visit_image - model_field
    return lax.map(per_visit, (science, weights, grams))
```

```python
import functools

import jax
import jax.numpy as jnp
from jax import lax
from jax.experimental import pallas as pl
from jax.experimental.pallas import tpu as pltpu
from jax.sharding import PartitionSpec as P

S = 32
GROUP = 16
EDGE = 16
LANES = 128
HALF = LANES // 2
BLOCK = 8
PIECES = 2
ridge_weight = 1.0
F32 = jnp.float32
BF16 = jnp.bfloat16
NT = (((1,), (1,)), ((), ()))
NN = (((1,), (0,)), ((), ()))


def split(value):
    high = value.astype(BF16)
    return high, (value - high.astype(F32)).astype(BF16)


def iota(shape, axis):
    return lax.broadcasted_iota(jnp.int32, shape, axis)


def shifted(value, turn):
    turn %= value.shape[1]
    return pltpu.roll(value, turn, 1) if turn else value


def toeplitz(profile_row, rows):
    width = profile_row.shape[1]
    base = pltpu.roll(jnp.broadcast_to(profile_row, (8, width)), 0, 1, stride=1, stride_axis=0)
    return jnp.concatenate([shifted(base, first) for first in range(0, rows, 8)], axis=0)


def xi_row(cols, total):
    start = lax.axis_index("tile") * cols
    return 2.0 * (start + iota((1, cols), 1)).astype(F32) / total - 1.0


def chunk_rows(rows, own, extra):
    sizes = [r for r in range(16, LANES - extra + 1, 16) if rows % r == 0 and r % own == 0]
    return max(sizes)


def make_bands(rowp_ref, colp_ref, profile_ref, row_band_ref, col_band_ref, shift):
    count, taps = rowp_ref.shape
    seg = HALF + taps - 1
    profile_ref[...] = jnp.zeros_like(profile_ref)
    high, low = (part.astype(F32) for part in split(rowp_ref[...]))
    profile_ref[0, :count, shift : shift + taps] = high
    profile_ref[0, :count, LANES + shift : LANES + shift + taps] = low
    high, low = (part.astype(F32) for part in split(colp_ref[...]))
    profile_ref[1, :count, :taps] = high
    profile_ref[1, :count, seg : seg + taps] = high
    profile_ref[1, :count, 2 * seg : 2 * seg + taps] = low
    for b in range(count):
        row_band_ref[b] = toeplitz(profile_ref[0, b : b + 1, :], row_band_ref.shape[1]).astype(BF16)
        col_band_ref[b] = toeplitz(profile_ref[1, b : b + 1, :], HALF).astype(BF16)


def window_terms(window, seg):
    lane = iota((1, LANES), 1)
    high = window.astype(BF16).astype(F32)
    low = shifted(window - high, seg)
    first = jnp.where(lane < seg, high, low)
    second = jnp.where(lane < 2 * seg - LANES, low, shifted(high, 2 * seg))
    return jnp.concatenate([first, second], axis=1).astype(BF16)


def column_pass(own, beside, at, taps, col_band_ref, across_ref):
    count = across_ref.shape[0]
    rows = own.shape[0]
    half = taps // 2
    seg = HALF + taps - 1
    lane = iota((1, LANES), 1)
    left = jnp.where(lane < half, shifted(beside, half - EDGE), jnp.where(lane < seg, shifted(own, half), 0.0))
    cut = HALF + half
    right = jnp.where(lane < cut, shifted(own, half - HALF), jnp.where(lane < seg, shifted(beside, cut - EDGE), 0.0))
    terms = jnp.concatenate([window_terms(left, seg), window_terms(right, seg)], axis=0)
    for first in range(0, count, 4):
        members = [b for b in range(first, first + 4) if b < count]
        band = jnp.concatenate([col_band_ref[b] for b in members], axis=0)
        both = lax.dot_general(terms, band, NT, preferred_element_type=F32)
        for k in range(0, len(members), 2):
            low, high = both[:rows, k * HALF : k * HALF + LANES], both[rows:, k * HALF : k * HALF + LANES]
            if low.shape[1] < LANES:
                spare = jnp.zeros((rows, LANES - low.shape[1]), F32)
                low, high = (jnp.concatenate([v, spare], axis=1) for v in (low, high))
            joined = [jnp.where(lane < HALF, low, shifted(high, HALF)), jnp.where(lane < HALF, shifted(low, HALF), high)]
            for b, across in zip(members[k : k + 2], joined):
                across_ref[b, at, :] = jnp.concatenate(split(across), axis=1)


def row_pass(start, row_band_ref, across_ref, images_ref, pitch):
    count = across_ref.shape[0]
    size = row_band_ref.shape[1]
    window = pl.ds(pl.multiple_of(start, 16), LANES)
    spare = jnp.zeros((LANES, LANES), BF16)
    for b in range(count):
        across = across_ref[b, window, :]
        under = jnp.concatenate([across[:, :LANES], spare], axis=1)
        both = lax.dot_general(
            row_band_ref[b], jnp.concatenate([across, under], axis=0), NN, preferred_element_type=F32
        )
        images_ref[pl.ds(b * pitch + start, size), :] = both[:, :LANES] + both[:, LANES:]


def make_weight(srow_ref, scol_ref, cov_ref, root_ref):
    _, rows, cols = root_ref.shape
    stamps = srow_ref.shape[1]
    at = iota((cols, stamps), 0) - scol_ref[...]
    cols_in = jnp.where((at >= 0) & (at < S), cov_ref[...].astype(F32), 0.0).astype(BF16)
    at = iota((rows, stamps), 0) - srow_ref[...]
    rows_in = jnp.where((at >= 0) & (at < S), 1.0, 0.0).astype(BF16)
    root = jnp.sqrt(lax.dot_general(rows_in, cols_in, NT, preferred_element_type=F32))
    root_ref[0] = root
    root_ref[1] = root * (2.0 * iota((rows, 1), 0).astype(F32) / rows - 1.0)


def gram(start, size, root_ref, images_ref, total_ref, pitch, total):
    cols = images_ref.shape[1]
    xi = xi_row(cols, total)
    plain, across, down = [], [], []
    for j in range(size):
        y = start + j
        feature = jnp.concatenate(
            [images_ref[pl.ds(first * pitch + y, 8, stride=pitch), :] for first in range(0, GROUP, 8)], axis=0
        )
        scaled = feature * root_ref[0, pl.ds(y, 1), :]
        plain.append(scaled)
        across.append(scaled * xi)
        down.append(feature * root_ref[1, pl.ds(y, 1), :])
    feats = jnp.concatenate([jnp.concatenate(v, axis=1) for v in (plain, across, down)], axis=0)
    high, low = split(feats)
    both = jnp.concatenate([high, low], axis=0)
    total_ref[...] += lax.dot_general(high, both, NT, preferred_element_type=F32)


def combine(total_ref):
    side = 3 * GROUP
    spare = jnp.zeros((side, LANES - side), F32)
    sums = total_ref[...]
    mixed = jnp.concatenate([sums[:, side:], spare], axis=1)
    turned = jnp.transpose(jnp.concatenate([mixed, jnp.zeros((LANES - side, LANES), F32)], axis=0))
    return jnp.concatenate([sums[:, :side], spare], axis=1) + (mixed + turned[:side])


def solve(normal, count):
    side = 3 * GROUP
    row, col = iota((side, LANES), 0), iota((side, LANES), 1)

    def used(k):
        return ((k % GROUP < count) & (k < side)) | (k == count)

    rhs = normal[:, count + 1 : count + 2]
    system = jnp.where(used(row) & used(col), normal, 0.0) + ridge_weight * jnp.where(row == col, 1.0, 0.0)
    system = jnp.where((col == side) & used(row), rhs, system)
    unknowns = [k for k in range(side) if (k % GROUP < count) or k == count]
    scale = jnp.zeros((side, LANES), F32)
    for first in range(0, len(unknowns), BLOCK):
        block = unknowns[first : first + BLOCK]
        columns = [jnp.broadcast_to(system[:, p : p + 1], (side, LANES)) for p in block]
        for k, p in enumerate(block):
            column = columns[k]
            inverse = 1.0 / column[p : p + 1, :]
            scale = jnp.where(row == p, inverse, scale)
            factor = jnp.where(row == p, 0.0, column)
            for later in range(k + 1, len(block)):
                columns[later] = columns[later] - factor * (columns[later][p : p + 1, :] * inverse)
            system = system - factor * (system[p : p + 1, :] * inverse)
    return jnp.broadcast_to(system[:, side : side + 1], (side, LANES)) * scale


def apply(coefs, images_ref, science_ref, out_ref, pitch, count, total):
    _, rows, cols = science_ref.shape
    xi = xi_row(cols, total)
    wide = lambda k: jnp.broadcast_to(coefs[k : k + 1, :], (8, cols))
    flat = [wide(b) + wide(GROUP + b) * xi for b in range(count)]
    slope = [wide(2 * GROUP + b) for b in range(count)]
    constant = wide(count)
    step = 4 if rows % 32 == 0 else 1

    def body(turn, carry):
        for k in range(step):
            start = pl.multiple_of((turn * step + k) * 8, 8)
            eta = 2.0 * (start + iota((8, cols), 0)).astype(F32) / rows - 1.0
            field = constant
            for b in range(count):
                field = field + images_ref[pl.ds(b * pitch + start, 8), :] * (flat[b] + slope[b] * eta)
            out_ref[0, pl.ds(start, 8), :] = science_ref[0, pl.ds(start, 8), :] - field
        return carry

    lax.fori_loop(0, rows // (8 * step), body, 0)


def remote(source, target, send, recv, epoch, tile):
    return pltpu.make_async_remote_copy(
        src_ref=source,
        dst_ref=target,
        send_sem=send,
        recv_sem=recv,
        device_id={"epoch": epoch, "tile": tile},
        device_id_type=pl.DeviceIdType.MESH,
    )


def kernel(total, top, pitch, template_in, science_in, rowp_in, colp_in, cov_in, srow_in, scol_in, out_ref,
           science_ref, rowp_ref, colp_ref, cov_ref, srow_ref, scol_ref,
           slots, pack, edges, across_ref, parts, mine, images_ref, root_ref, total_ref, profile_ref,
           row_band_ref, col_band_ref, slot_send, slot_recv, edge_send, edge_recv, side_send, side_recv,
           part_send, part_recv, load_sem):
    count, taps = rowp_ref.shape
    _, rows, cols = science_ref.shape
    epochs, own_rows, _ = slots.shape
    tiles = parts.shape[0]
    pieces = slot_recv.shape[1]
    size = row_band_ref.shape[1]
    epoch, tile = lax.axis_index("epoch"), lax.axis_index("tile")

    loads = [
        pltpu.make_async_copy(source, target, load_sem.at[k])
        for k, (source, target) in enumerate(
            [
                (template_in, slots.at[epoch]),
                (rowp_in, rowp_ref),
                (colp_in, colp_ref),
                (cov_in, cov_ref),
                (srow_in, srow_ref),
                (scol_in, scol_ref),
                (science_in, science_ref),
            ]
        )
    ]
    for load in loads:
        load.start()
    barrier = pltpu.get_barrier_semaphore()
    ahead, behind = epoch < epochs - 1, epoch > 0

    def greet(e, t):
        pl.semaphore_signal(barrier, inc=1, device_id={"epoch": e, "tile": t}, device_id_type=pl.DeviceIdType.MESH)

    for t in range(1, tiles):
        greet(epoch, lax.rem(tile + t, tiles))

    @pl.when(behind)
    def _():
        greet(epoch - 1, tile)

    @pl.when(ahead)
    def _():
        greet(epoch + 1, tile)

    loads[0].wait()
    flipped = jnp.transpose(slots[epoch])
    pack[0] = flipped[:EDGE]
    pack[1] = flipped[cols - EDGE :]
    pl.semaphore_wait(barrier, tiles - 1 + behind.astype(jnp.int32) + ahead.astype(jnp.int32))

    def block_copy(direction, source, piece):
        part = pl.ds(piece * (own_rows // pieces), own_rows // pieces)
        return remote(slots.at[source, part], slots.at[source, part], slot_send.at[direction, source, piece],
                      slot_recv.at[source, piece], epoch + 2 * direction - 1, tile)

    def edge_copy(direction, source):
        return remote(edges.at[source], edges.at[source], edge_send.at[direction, source], edge_recv.at[source],
                      epoch + 2 * direction - 1, tile)

    def side_copy(side):
        place = pl.ds((1 - side) * EDGE, EDGE)
        return remote(pack.at[side], edges.at[epoch, place], side_send.at[side], side_recv.at[1 - side],
                      epoch, tile + 2 * side - 1)

    has_left, has_right = tile > 0, tile < tiles - 1
    for direction, there in ((0, behind), (1, ahead)):

        @pl.when(there)
        def _():
            for piece in range(pieces):
                block_copy(direction, epoch, piece).start()

    for side, there in ((0, has_left), (1, has_right)):

        @pl.when(there)
        def _():
            side_copy(side).start()

        @pl.when(jnp.logical_not(there))
        def _():
            edges[epoch, side * EDGE : (side + 1) * EDGE, :] = jnp.zeros((EDGE, own_rows), F32)

    for load in loads[1:]:
        load.wait()
    make_bands(rowp_ref, colp_ref, profile_ref, row_band_ref, col_band_ref, top - taps // 2)
    high = across_ref.shape[1]
    across_ref[:, :top, :] = jnp.zeros((count, top, 2 * cols), BF16)
    across_ref[:, top + rows :, :] = jnp.zeros((count, high - top - rows, 2 * cols), BF16)

    for side, there in ((0, has_left), (1, has_right)):

        @pl.when(there)
        def _():
            side_copy(1 - side).wait_recv()

    for direction, there in ((0, behind), (1, ahead)):

        @pl.when(there)
        def _():
            edge_copy(direction, epoch).start()

    make_weight(srow_ref, scol_ref, cov_ref, root_ref)
    images_ref[pl.ds(count * pitch, rows), :] = jnp.ones((rows, cols), F32)
    images_ref[pl.ds((count + 1) * pitch, rows), :] = science_ref[0]
    for spare in range(count + 2, GROUP):
        images_ref[pl.ds(spare * pitch, rows), :] = jnp.zeros((rows, cols), F32)
    total_ref[...] = jnp.zeros_like(total_ref)

    each = size // own_rows
    middle = jnp.zeros((cols - 2 * EDGE, own_rows), F32)

    def columns(chunk):
        owns = [slots[chunk * each + k] for k in range(each)]
        sides = [jnp.transpose(jnp.concatenate([edges[chunk * each + k], middle], axis=0)) for k in range(each)]
        at = pl.ds(pl.multiple_of(top + chunk * size, 16), size)
        column_pass(jnp.concatenate(owns, axis=0), jnp.concatenate(sides, axis=0), at, taps, col_band_ref, across_ref)

    def chunk_work(chunk):
        start = pl.multiple_of(chunk * size, 16)
        row_pass(start, row_band_ref, across_ref, images_ref, pitch)
        gram(start, size, root_ref, images_ref, total_ref, pitch, total)

    def arrive(source, onward):
        direction = jnp.int32(onward)
        for piece in range(pieces):
            block_copy(direction, source, piece).wait_recv()

            @pl.when(ahead if onward else behind)
            def _():
                block_copy(direction, source, piece).start()

        edge_copy(direction, source).wait_recv()

        @pl.when(ahead if onward else behind)
        def _():
            edge_copy(direction, source).start()

    def step(d, carry):
        was_low, was_high = carry
        left, right = epoch - d, epoch + d
        has_before, has_after = (left >= 0) & (d > 0), (right < epochs) & (d > 0)

        @pl.when(has_before)
        def _():
            arrive(left, 1)

        @pl.when(has_after)
        def _():
            arrive(right, 0)

        if each > 1:
            return carry

        def fresh(k, carry):
            columns(jnp.where((k == 0) & (left >= 0), left, right))
            return carry

        lax.fori_loop(0, jnp.where(d == 0, 1, has_before.astype(jnp.int32) + has_after.astype(jnp.int32)), fresh, 0)
        low, high = jnp.maximum(left, 0), jnp.minimum(right, epochs - 1)
        low, high = jnp.where(low > 0, low + 1, low), jnp.where(high < epochs - 1, high, high + 1)
        low, high = jnp.where(low < high, low, epoch), jnp.where(low < high, high, epoch)
        under = was_low - low

        def ready(k, carry):
            chunk_work(jnp.where(k < under, was_low - 1 - k, was_high + k - under))
            return carry

        lax.fori_loop(0, under + high - was_high, ready, 0)
        return low, high

    lax.fori_loop(0, epochs, step, (epoch, epoch))
    if each > 1:

        def fresh_chunk(chunk, carry):
            columns(chunk)
            return carry

        def ready_chunk(chunk, carry):
            chunk_work(chunk)
            return carry

        lax.fori_loop(0, rows // size, fresh_chunk, 0)
        lax.fori_loop(0, rows // size, ready_chunk, 0)

    normal = combine(total_ref)
    side = 3 * GROUP
    normal = normal[: side // 2] + shifted(normal[side // 2 :], HALF)
    mine[...] = normal

    def part_copy(t, source):
        return remote(mine, parts.at[source], part_send.at[t], part_recv.at[source],
                      epoch, lax.rem(tile + t, tiles))

    for t in range(1, tiles):
        part_copy(t, tile).start()
    for t in range(1, tiles):
        source = lax.rem(tile + tiles - t, tiles)
        part_copy(t, source).wait_recv()
        normal = normal + parts[source]
    for t in range(1, tiles):
        part_copy(t, tile).wait_send()

    for s, there in ((0, has_left), (1, has_right)):

        @pl.when(there)
        def _():
            side_copy(s).wait_send()

    for direction, there in ((0, behind), (1, ahead)):

        def sent(source, carry):
            for piece in range(pieces):
                block_copy(direction, source, piece).wait_send()
            edge_copy(direction, source).wait_send()
            return carry

        @pl.when(there)
        def _():
            lax.fori_loop(*((0, epoch + 1) if direction else (epoch, epochs)), sent, 0)

    lane = iota((1, LANES), 1)
    normal = jnp.concatenate(
        [jnp.where(lane < HALF, normal, 0.0), jnp.where(lane < HALF, shifted(normal, HALF), 0.0)], axis=0
    )
    coefs = solve(normal, count)
    apply(coefs, images_ref, science_ref, out_ref, pitch, count, total)


def local(template, science, row_profiles, col_profiles, coverage, stamp_rows, stamp_cols):
    count, taps = row_profiles.shape
    rows, cols = science.shape[1:]
    own_rows = template.shape[0]
    tiles, epochs = lax.axis_size("tile"), lax.axis_size("epoch")
    top = -(-(taps // 2) // 16) * 16
    size = chunk_rows(rows, own_rows, taps - 1 + top - taps // 2)
    pitch = rows + 4
    pieces = PIECES if own_rows % (8 * PIECES) == 0 else 1
    vmem = pl.BlockSpec(memory_space=pltpu.VMEM)
    dma = pltpu.SemaphoreType.DMA
    operands = (
        template,
        science,
        row_profiles,
        col_profiles,
        coverage,
        stamp_rows.reshape(1, -1),
        stamp_cols.reshape(1, -1),
    )
    return pl.pallas_call(
        functools.partial(kernel, cols * tiles, top, pitch),
        out_shape=jax.ShapeDtypeStruct(science.shape, F32),
        in_specs=[pl.BlockSpec(memory_space=pl.ANY)] * 7,
        out_specs=vmem,
        scratch_shapes=[
            pltpu.VMEM(science.shape, F32),
            pltpu.VMEM(row_profiles.shape, F32),
            pltpu.VMEM(col_profiles.shape, F32),
            pltpu.VMEM(coverage.shape, jnp.int32),
            pltpu.VMEM((1, stamp_rows.shape[0]), jnp.int32),
            pltpu.VMEM((1, stamp_cols.shape[0]), jnp.int32),
            pltpu.VMEM((epochs, own_rows, cols), F32),
            pltpu.VMEM((2, EDGE, own_rows), F32),
            pltpu.VMEM((epochs, 2 * EDGE, own_rows), F32),
            pltpu.VMEM((count, rows - size + LANES, 2 * cols), BF16),
            pltpu.VMEM((tiles, 3 * GROUP // 2, LANES), F32),
            pltpu.VMEM((3 * GROUP // 2, LANES), F32),
            pltpu.VMEM((GROUP * pitch, cols), F32),
            pltpu.VMEM((2, rows, cols), F32),
            pltpu.VMEM((3 * GROUP, 6 * GROUP), F32),
            pltpu.VMEM((2, GROUP, 2 * LANES), F32),
            pltpu.VMEM((count, size, 2 * LANES), BF16),
            pltpu.VMEM((count, HALF, 2 * LANES), BF16),
            dma((2, epochs, pieces)),
            dma((epochs, pieces)),
            dma((2, epochs)),
            dma((epochs,)),
            dma((2,)),
            dma((2,)),
            dma((tiles,)),
            dma((tiles,)),
            dma((7,)),
        ],
        compiler_params=pltpu.CompilerParams(
            collective_id=0, has_side_effects=True, vmem_limit_bytes=48 * 2**20
        ),
    )(*(pltpu.with_memory_space_constraint(operand, pltpu.HBM) for operand in operands))


def solution(mesh):
    in_specs = (
        P(("patch", "epoch"), "tile"),
        P(("patch", "epoch"), None, "tile"),
        P(),
        P(),
        P(("patch", "epoch"), "tile"),
        P(("patch", "tile")),
        P(("patch", "tile")),
    )
    out_specs = P(("patch", "epoch"), None, "tile")
    return jax.shard_map(local, mesh=mesh, in_specs=in_specs, out_specs=out_specs, check_vma=False)
```

```python
import functools

import jax
import jax.numpy as jnp
from jax import lax
from jax.experimental import pallas as pl
from jax.experimental.pallas import tpu as pltpu
from jax.sharding import PartitionSpec as P

S = 32
GROUP = 16
EDGE = 16
LANES = 128
HALF = LANES // 2
BLOCK = 8
SIDE = 40
TURN = 16
FOLD = 24
DUAL = 48
BOTH = 80
ridge_weight = 1.0
F32 = jnp.float32
BF16 = jnp.bfloat16
NT = (((1,), (1,)), ((), ()))
NN = (((1,), (0,)), ((), ()))


def split(value):
    high = value.astype(BF16)
    return high, (value - high.astype(F32)).astype(BF16)


def iota(shape, axis):
    return lax.broadcasted_iota(jnp.int32, shape, axis)


def shifted(value, turn):
    turn %= value.shape[1]
    return pltpu.roll(value, turn, 1) if turn else value


def toeplitz(profile_row, rows, turn=0):
    width = profile_row.shape[1]
    base = pltpu.roll(jnp.broadcast_to(profile_row, (8, width)), 0, 1, stride=1, stride_axis=0)
    return jnp.concatenate([shifted(base, turn + first) for first in range(0, rows, 8)], axis=0)


def xi_row(cols, total):
    start = lax.axis_index("tile") * cols
    return 2.0 * (start + iota((1, cols), 1)).astype(F32) / total - 1.0


def chunk_rows(rows, own, extra):
    sizes = [r for r in range(16, LANES - extra + 1, 16) if rows % r == 0 and r % own == 0]
    return max(sizes)


def make_bands(rowp_ref, colp_ref, profile_ref, row_band_ref, col_band_ref, shift):
    count, taps = rowp_ref.shape
    half = taps // 2
    profile_ref[...] = jnp.zeros_like(profile_ref)
    high, low = (part.astype(F32) for part in split(rowp_ref[...]))
    profile_ref[0, :count, shift : shift + taps] = high
    profile_ref[0, :count, LANES + shift : LANES + shift + taps] = low
    flip = jnp.where(iota((taps, taps), 0) + iota((taps, taps), 1) == taps - 1, 1.0, 0.0).astype(BF16)
    for k, part in enumerate(split(colp_ref[...])):
        profile_ref[1 + k, :count, :taps] = lax.dot_general(part, flip, NN, preferred_element_type=F32)
    gap = jnp.zeros((LANES - 6 * EDGE, LANES), BF16)
    for b in range(count):
        row_band_ref[b] = toeplitz(profile_ref[0, b : b + 1, :], row_band_ref.shape[1]).astype(BF16)
        parts = []
        for k in (1, 2):
            tall = toeplitz(profile_ref[k, b : b + 1, :], LANES + 2 * EDGE, -half - EDGE)[:, :LANES].astype(BF16)
            beside = jnp.concatenate([tall[:EDGE], tall[EDGE + LANES :]], axis=0)
            parts.append((tall[EDGE : EDGE + LANES], beside))
        (high, near_high), (low, near_low) = parts
        at = pl.ds((b % 2) * LANES, LANES)
        column = jnp.concatenate([high, high, low, near_high, near_high, near_low, gap], axis=0)
        col_band_ref[b // 2, :, at] = column


def column_pass(own, beside, at, col_band_ref, across_ref):
    count = across_ref.shape[0]
    lane = iota((1, LANES), 1)
    high, low = split(own)
    near = jnp.where(lane < 2 * EDGE, beside, 0.0)
    near_high = near.astype(BF16).astype(F32)
    near_low = near - near_high
    near = near_high + shifted(near_low, 2 * EDGE) + shifted(near_high, 4 * EDGE)
    terms = jnp.concatenate([high, low, high, near.astype(BF16)], axis=1)
    for pair in range(0, count, 2):
        both = lax.dot_general(terms, col_band_ref[pair // 2], NN, preferred_element_type=F32)
        for k, b in enumerate(range(pair, min(pair + 2, count))):
            across_ref[b, at, :] = jnp.concatenate(split(both[:, k * LANES : (k + 1) * LANES]), axis=1)


def row_pass(start, row_band_ref, across_ref, images_ref, pitch):
    count = across_ref.shape[0]
    size = row_band_ref.shape[1]
    window = pl.ds(pl.multiple_of(start, 16), LANES)
    spare = jnp.zeros((LANES, LANES), BF16)
    for b in range(count):
        across = across_ref[b, window, :]
        under = jnp.concatenate([across[:, :LANES], spare], axis=1)
        both = lax.dot_general(
            row_band_ref[b], jnp.concatenate([across, under], axis=0), NN, preferred_element_type=F32
        )
        images_ref[pl.ds(b * pitch + start, size), :] = both[:, :LANES] + both[:, LANES:]


def make_weight(srow_ref, scol_ref, cov_ref, root_ref, total):
    _, rows, cols = root_ref.shape
    stamps = srow_ref.shape[1]
    at = iota((cols, stamps), 0) - scol_ref[...]
    cols_in = jnp.where((at >= 0) & (at < S), cov_ref[...].astype(F32), 0.0).astype(BF16)
    at = iota((rows, stamps), 0) - srow_ref[...]
    rows_in = jnp.where((at >= 0) & (at < S), 1.0, 0.0).astype(BF16)
    root = jnp.sqrt(lax.dot_general(rows_in, cols_in, NT, preferred_element_type=F32))
    root_ref[0] = root
    root_ref[1] = root * xi_row(cols, total)
    root_ref[2] = root * (2.0 * iota((rows, 1), 0).astype(F32) / rows - 1.0)


def gram(start, size, root_ref, images_ref, first_ref, second_ref, pitch):
    upper = iota((8, images_ref.shape[1]), 0) < 4

    def row(j):
        y = start + j
        low, high, cross = (images_ref[pl.ds(k * pitch + y, 8, stride=pitch), :] for k in (0, 8, 4))
        plain, by_xi, by_eta = (jnp.broadcast_to(root_ref[k, pl.ds(y, 1), :], low.shape) for k in range(3))
        body = jnp.concatenate([low * plain, high * plain, low * by_xi, low * by_eta], axis=0)
        return body, jnp.where(upper, high, cross) * jnp.where(upper, by_xi, by_eta)

    def terms(first, last):
        body, rest = (jnp.concatenate(v, axis=1) for v in zip(*[row(j) for j in range(first, last)]))
        high, low = split(body)
        rest = jnp.concatenate([rest, rest - rest.astype(BF16).astype(F32)], axis=0).astype(BF16)
        short = jnp.concatenate([high, rest], axis=0)
        return short, jnp.concatenate([short, low], axis=0)

    first, second = first_ref[...], second_ref[...]
    for turn in range(0, size, TURN):
        short, whole = terms(turn, turn + TURN // 2)
        first = first + lax.dot_general(short, whole, NT, preferred_element_type=F32)
        short, whole = terms(turn + TURN // 2, turn + TURN)
        second = second + lax.dot_general(whole, short, NT, preferred_element_type=F32)
    first_ref[...], second_ref[...] = first, second


def combine(first_ref, second_ref):
    def pad(value, rows=SIDE):
        value = jnp.concatenate([value, jnp.zeros((value.shape[0], LANES - value.shape[1]), F32)], axis=1)
        if rows == value.shape[0]:
            return value
        return jnp.concatenate([value, jnp.zeros((rows - value.shape[0], LANES), F32)], axis=0)

    first, second = first_ref[:SIDE], second_ref[:, :SIDE]
    mixed = jnp.concatenate([first[:, DUAL:], first[:, SIDE:DUAL]], axis=1)
    mixed = mixed + jnp.concatenate([second[DUAL:], second[SIDE:DUAL]], axis=0)
    turned = jnp.transpose(pad(mixed, LANES))[:SIDE]
    return pad(first[:, :SIDE] + second[:SIDE]) + (pad(mixed) + turned)


def place(kind, b):
    if kind == 0:
        return b
    return (8 + 8 * kind + b) if b < 8 else (28 + 4 * kind + b - 8)


def solve(normal, count):
    side = SIDE
    row, col = iota((side, LANES), 0), iota((side, LANES), 1)
    unknowns = sorted([place(kind, b) for kind in range(3) for b in range(count)] + [count])

    def used(k):
        spare = [p for p in range(side) if p not in unknowns]
        keep = k < side
        for p in spare:
            keep = keep & (k != p)
        return keep

    rhs = normal[:, count + 1 : count + 2]
    system = jnp.where(used(row) & used(col), normal, 0.0) + ridge_weight * jnp.where(row == col, 1.0, 0.0)
    system = jnp.where((col == side) & used(row), rhs, system)
    scale = jnp.zeros((side, LANES), F32)
    for first in range(0, len(unknowns), BLOCK):
        block = unknowns[first : first + BLOCK]
        columns = [jnp.broadcast_to(system[:, p : p + 1], (side, LANES)) for p in block]
        for k, p in enumerate(block):
            column = columns[k]
            inverse = 1.0 / column[p : p + 1, :]
            scale = jnp.where(row == p, inverse, scale)
            factor = jnp.where(row == p, 0.0, column)
            for later in range(k + 1, len(block)):
                columns[later] = columns[later] - factor * (columns[later][p : p + 1, :] * inverse)
            system = system - factor * (system[p : p + 1, :] * inverse)
    return jnp.broadcast_to(system[:, side : side + 1], (side, LANES)) * scale


def apply(coefs, images_ref, science_ref, out_ref, pitch, count, total):
    _, rows, cols = science_ref.shape
    xi = xi_row(cols, total)
    wide = lambda k: jnp.broadcast_to(coefs[k : k + 1, :], (8, cols))
    flat = [wide(b) + wide(place(1, b)) * xi for b in range(count)]
    slope = [wide(place(2, b)) for b in range(count)]
    constant = wide(count)
    step = 4 if rows % 32 == 0 else 1

    def body(turn, carry):
        for k in range(step):
            start = pl.multiple_of((turn * step + k) * 8, 8)
            eta = 2.0 * (start + iota((8, cols), 0)).astype(F32) / rows - 1.0
            field = constant
            for b in range(count):
                field = field + images_ref[pl.ds(b * pitch + start, 8), :] * (flat[b] + slope[b] * eta)
            out_ref[0, pl.ds(start, 8), :] = science_ref[0, pl.ds(start, 8), :] - field
        return carry

    lax.fori_loop(0, rows // (8 * step), body, 0)


def remote(source, target, send, recv, epoch, tile):
    return pltpu.make_async_remote_copy(
        src_ref=source,
        dst_ref=target,
        send_sem=send,
        recv_sem=recv,
        device_id={"epoch": epoch, "tile": tile},
        device_id_type=pl.DeviceIdType.MESH,
    )


def kernel(total, top, pitch, template_in, science_in, rowp_in, colp_in, cov_in, srow_in, scol_in, out_ref,
           science_ref, rowp_ref, colp_ref, cov_ref, srow_ref, scol_ref,
           slots, pack, edges, across_ref, parts, mine, images_ref, root_ref, first_ref, second_ref, profile_ref,
           row_band_ref, col_band_ref, slot_send, slot_recv, edge_send, edge_recv,
           part_send, part_recv, load_sem, hello):
    count, taps = rowp_ref.shape
    _, rows, cols = science_ref.shape
    epochs, own_rows, _ = slots.shape
    tiles = parts.shape[0]
    size = row_band_ref.shape[1]
    epoch, tile = lax.axis_index("epoch"), lax.axis_index("tile")

    loads = [
        pltpu.make_async_copy(source, target, load_sem.at[k])
        for k, (source, target) in enumerate(
            [
                (template_in, slots.at[epoch]),
                (rowp_in, rowp_ref),
                (colp_in, colp_ref),
                (cov_in, cov_ref),
                (srow_in, srow_ref),
                (scol_in, scol_ref),
                (science_in, science_ref),
            ]
        )
    ]
    for load in loads:
        load.start()
    barrier = pltpu.get_barrier_semaphore()
    has_left, has_right = tile > 0, tile < tiles - 1

    def greet(semaphore, e, t):
        pl.semaphore_signal(semaphore, inc=1, device_id={"epoch": e, "tile": t}, device_id_type=pl.DeviceIdType.MESH)

    for t in range(1, tiles):
        greet(barrier, epoch, lax.rem(tile + t, tiles))

    def greet_above(target, carry):
        greet(barrier, target, tile)

        @pl.when(has_left)
        def _():
            greet(barrier, target, tile - 1)

        @pl.when(has_right)
        def _():
            greet(barrier, target, tile + 1)

        return carry

    lax.fori_loop(epoch + 1, epochs, greet_above, 0)
    loads[0].wait()
    flipped = jnp.transpose(slots[epoch])
    pack[0] = flipped[:EDGE]
    pack[1] = flipped[cols - EDGE :]
    around = 1 + has_left.astype(jnp.int32) + has_right.astype(jnp.int32)
    pl.semaphore_wait(barrier, tiles - 1 + epoch * around)

    def announce(target, carry):
        greet(hello.at[epoch], target, tile)
        return carry

    lax.fori_loop(0, epoch, announce, 0)

    def block_copy(target, source):
        return remote(template_in, slots.at[source], slot_send.at[target], slot_recv.at[source], target, tile)

    def edge_copy(target, side, source):
        place = pl.ds((1 - side) * EDGE, EDGE)
        return remote(pack.at[side], edges.at[source, place], edge_send.at[side, target], edge_recv.at[1 - side, source],
                      target, tile + 2 * side - 1)

    def send(target, carry):
        for side, there in ((0, has_left), (1, has_right)):

            @pl.when(there)
            def _():
                edge_copy(target, side, epoch).start()

        @pl.when(target != epoch)
        def _():
            block_copy(target, epoch).start()

        return carry

    def send_up(target):
        @pl.when(target < epochs)
        def _():
            pl.semaphore_wait(hello.at[target], 1)
            send(target, 0)

    lax.fori_loop(0, epoch + 1, send, 0)

    for side, there in ((0, has_left), (1, has_right)):

        @pl.when(jnp.logical_not(there))
        def _():
            edges[:, side * EDGE : (side + 1) * EDGE, :] = jnp.zeros((epochs, EDGE, own_rows), F32)

    for load in loads[1:]:
        load.wait()
    make_bands(rowp_ref, colp_ref, profile_ref, row_band_ref, col_band_ref, top - taps // 2)
    high = across_ref.shape[1]
    send_up(epoch + 1)
    across_ref[:, :top, :] = jnp.zeros((count, top, 2 * cols), BF16)
    across_ref[:, top + rows :, :] = jnp.zeros((count, high - top - rows, 2 * cols), BF16)

    make_weight(srow_ref, scol_ref, cov_ref, root_ref, total)
    images_ref[pl.ds(count * pitch, rows), :] = jnp.ones((rows, cols), F32)
    images_ref[pl.ds((count + 1) * pitch, rows), :] = science_ref[0]
    for spare in range(count + 2, GROUP):
        images_ref[pl.ds(spare * pitch, rows), :] = jnp.zeros((rows, cols), F32)
    first_ref[...] = jnp.zeros_like(first_ref)
    second_ref[...] = jnp.zeros_like(second_ref)

    each = size // own_rows
    middle = jnp.zeros((cols - 2 * EDGE, own_rows), F32)

    def columns(chunk):
        owns = [slots[chunk * each + k] for k in range(each)]
        sides = [jnp.transpose(jnp.concatenate([edges[chunk * each + k], middle], axis=0)) for k in range(each)]
        at = pl.ds(pl.multiple_of(top + chunk * size, 16), size)
        column_pass(jnp.concatenate(owns, axis=0), jnp.concatenate(sides, axis=0), at, col_band_ref, across_ref)

    def chunk_work(chunk):
        start = pl.multiple_of(chunk * size, 16)
        row_pass(start, row_band_ref, across_ref, images_ref, pitch)
        gram(start, size, root_ref, images_ref, first_ref, second_ref, pitch)

    def arrive(source):
        @pl.when(source != epoch)
        def _():
            block_copy(epoch, source).wait_recv()

        for side, there in ((0, has_left), (1, has_right)):

            @pl.when(there)
            def _():
                edge_copy(epoch, 1 - side, source).wait_recv()

    def step(d, carry):
        was_low, was_high = carry
        left, right = epoch - d, epoch + d
        has_before, has_after = (left >= 0) & (d > 0), right < epochs

        send_up(right + 2)

        @pl.when(has_before)
        def _():
            arrive(left)

        @pl.when(has_after)
        def _():
            arrive(right)

        if each > 1:
            return carry

        def fresh(k, carry):
            columns(jnp.where((k == 0) & has_before, left, right))
            return carry

        lax.fori_loop(0, has_before.astype(jnp.int32) + has_after.astype(jnp.int32), fresh, 0)
        low, high = jnp.maximum(left, 0), jnp.minimum(right, epochs - 1)
        low, high = jnp.where(low > 0, low + 1, low), jnp.where(high < epochs - 1, high, high + 1)
        low, high = jnp.where(low < high, low, epoch), jnp.where(low < high, high, epoch)
        under = was_low - low

        def ready(k, carry):
            chunk_work(jnp.where(k < under, was_low - 1 - k, was_high + k - under))
            return carry

        lax.fori_loop(0, under + high - was_high, ready, 0)
        return low, high

    lax.fori_loop(0, epochs, step, (epoch, epoch))
    if each > 1:

        def fresh_chunk(chunk, carry):
            columns(chunk)
            return carry

        def ready_chunk(chunk, carry):
            chunk_work(chunk)
            return carry

        lax.fori_loop(0, rows // size, fresh_chunk, 0)
        lax.fori_loop(0, rows // size, ready_chunk, 0)

    normal = combine(first_ref, second_ref)
    under = jnp.concatenate([normal[FOLD:], jnp.zeros((2 * FOLD - SIDE, LANES), F32)], axis=0)
    normal = normal[:FOLD] + shifted(under, HALF)
    mine[...] = normal

    def part_copy(t, source):
        return remote(mine, parts.at[source], part_send.at[t], part_recv.at[source],
                      epoch, lax.rem(tile + t, tiles))

    for t in range(1, tiles):
        part_copy(t, tile).start()
    for t in range(1, tiles):
        source = lax.rem(tile + tiles - t, tiles)
        part_copy(t, source).wait_recv()
        normal = normal + parts[source]
    for t in range(1, tiles):
        part_copy(t, tile).wait_send()

    def sent(target, carry):
        @pl.when(target != epoch)
        def _():
            block_copy(target, epoch).wait_send()

        for side, there in ((0, has_left), (1, has_right)):

            @pl.when(there)
            def _():
                edge_copy(target, side, epoch).wait_send()

        return carry

    lax.fori_loop(0, epochs, sent, 0)
    lane = iota((1, LANES), 1)
    normal = jnp.concatenate(
        [jnp.where(lane < HALF, normal, 0.0), jnp.where(lane < HALF, shifted(normal, HALF), 0.0)[: SIDE - FOLD]], axis=0
    )
    coefs = solve(normal, count)
    apply(coefs, images_ref, science_ref, out_ref, pitch, count, total)


def local(template, science, row_profiles, col_profiles, coverage, stamp_rows, stamp_cols):
    count, taps = row_profiles.shape
    rows, cols = science.shape[1:]
    own_rows = template.shape[0]
    tiles, epochs = lax.axis_size("tile"), lax.axis_size("epoch")
    top = -(-(taps // 2) // 16) * 16
    size = chunk_rows(rows, own_rows, taps - 1 + top - taps // 2)
    pitch = rows + 4
    vmem = pl.BlockSpec(memory_space=pltpu.VMEM)
    dma = pltpu.SemaphoreType.DMA
    operands = (
        template,
        science,
        row_profiles,
        col_profiles,
        coverage,
        stamp_rows.reshape(1, -1),
        stamp_cols.reshape(1, -1),
    )
    return pl.pallas_call(
        functools.partial(kernel, cols * tiles, top, pitch),
        out_shape=jax.ShapeDtypeStruct(science.shape, F32),
        in_specs=[pl.BlockSpec(memory_space=pl.ANY)] * 7,
        out_specs=vmem,
        scratch_shapes=[
            pltpu.VMEM(science.shape, F32),
            pltpu.VMEM(row_profiles.shape, F32),
            pltpu.VMEM(col_profiles.shape, F32),
            pltpu.VMEM(coverage.shape, jnp.int32),
            pltpu.VMEM((1, stamp_rows.shape[0]), jnp.int32),
            pltpu.VMEM((1, stamp_cols.shape[0]), jnp.int32),
            pltpu.VMEM((epochs, own_rows, cols), F32),
            pltpu.VMEM((2, EDGE, own_rows), F32),
            pltpu.VMEM((epochs, 2 * EDGE, own_rows), F32),
            pltpu.VMEM((count, rows - size + LANES, 2 * cols), BF16),
            pltpu.VMEM((tiles, FOLD, LANES), F32),
            pltpu.VMEM((FOLD, LANES), F32),
            pltpu.VMEM((GROUP * pitch, cols), F32),
            pltpu.VMEM((3, rows, cols), F32),
            pltpu.VMEM((DUAL, BOTH), F32),
            pltpu.VMEM((BOTH, DUAL), F32),
            pltpu.VMEM((3, GROUP, 2 * LANES), F32),
            pltpu.VMEM((count, size, 2 * LANES), BF16),
            pltpu.VMEM((-(-count // 2), 4 * LANES, 2 * LANES), BF16),
            dma((epochs,)),
            dma((epochs,)),
            dma((2, epochs)),
            dma((2, epochs)),
            dma((tiles,)),
            dma((tiles,)),
            dma((7,)),
            pltpu.SemaphoreType.REGULAR((epochs,)),
        ],
        compiler_params=pltpu.CompilerParams(
            collective_id=0, has_side_effects=True, vmem_limit_bytes=48 * 2**20
        ),
    )(*(pltpu.with_memory_space_constraint(operand, pltpu.HBM) for operand in operands))


def solution(mesh):
    in_specs = (
        P(("patch", "epoch"), "tile"),
        P(("patch", "epoch"), None, "tile"),
        P(),
        P(),
        P(("patch", "epoch"), "tile"),
        P(("patch", "tile")),
        P(("patch", "tile")),
    )
    out_specs = P(("patch", "epoch"), None, "tile")
    return jax.shard_map(local, mesh=mesh, in_specs=in_specs, out_specs=out_specs, check_vma=False)
```

```python
import functools

import jax
import jax.numpy as jnp
from jax import lax
from jax.experimental import pallas as pl
from jax.experimental.pallas import tpu as pltpu
from jax.sharding import PartitionSpec as P

S = 32
GROUP = 16
EDGE = 16
LANES = 128
HALF = LANES // 2
BLOCK = 13
SIDE = 40
TURN = 8
FOLD = 24
DUAL = 48
BOTH = 80
ridge_weight = 1.0
F32 = jnp.float32
BF16 = jnp.bfloat16
NT = (((1,), (1,)), ((), ()))
NN = (((1,), (0,)), ((), ()))


def split(value):
    high = value.astype(BF16)
    return high, (value - high.astype(F32)).astype(BF16)


def iota(shape, axis):
    return lax.broadcasted_iota(jnp.int32, shape, axis)


def shifted(value, turn):
    turn %= value.shape[1]
    return pltpu.roll(value, turn, 1) if turn else value


def toeplitz(profile_row, rows, turn=0):
    width = profile_row.shape[1]
    base = pltpu.roll(jnp.broadcast_to(profile_row, (8, width)), 0, 1, stride=1, stride_axis=0)
    return jnp.concatenate([shifted(base, turn + first) for first in range(0, rows, 8)], axis=0)


def xi_row(cols, total):
    start = lax.axis_index("tile") * cols
    return 2.0 * (start + iota((1, cols), 1)).astype(F32) / total - 1.0


def unit_rows(rows, own, top):
    sizes = [r for r in range(16, 2 * LANES // 3 - 2 * top + 1, 16) if rows % (2 * r) == 0 and 2 * r % own == 0]
    return max(sizes)


def make_bands(rowp_ref, colp_ref, profile_ref, row_band_ref, col_band_ref, shift):
    count, taps = rowp_ref.shape
    half = taps // 2
    profile_ref[...] = jnp.zeros_like(profile_ref)
    high, low = (part.astype(F32) for part in split(rowp_ref[...]))
    _, size, width = row_band_ref.shape
    for k, part in enumerate((high, high, low)):
        at = k * (width // 3) + shift
        profile_ref[0, :count, at : at + taps] = part
    flip = jnp.where(iota((taps, taps), 0) + iota((taps, taps), 1) == taps - 1, 1.0, 0.0).astype(BF16)
    for k, part in enumerate(split(colp_ref[...])):
        profile_ref[1 + k, :count, :taps] = lax.dot_general(part, flip, NN, preferred_element_type=F32)
    gap = jnp.zeros((LANES - 6 * EDGE, LANES), BF16)
    for b in range(count):
        row_band_ref[b] = toeplitz(profile_ref[0, b : b + 1, :], size)[:, :width].astype(BF16)
        parts = []
        for k in (1, 2):
            tall = toeplitz(profile_ref[k, b : b + 1, :], LANES + 2 * EDGE, -half - EDGE)[:, :LANES].astype(BF16)
            beside = jnp.concatenate([tall[:EDGE], tall[EDGE + LANES :]], axis=0)
            parts.append((tall[EDGE : EDGE + LANES], beside))
        (high, near_high), (low, near_low) = parts
        at = pl.ds((b % 2) * LANES, LANES)
        column = jnp.concatenate([high, high, low, near_high, near_high, near_low, gap], axis=0)
        col_band_ref[b // 2, :, at] = column


def column_pass(own, beside, at, col_band_ref, across_ref):
    count = across_ref.shape[0]
    lane = iota((1, LANES), 1)
    high, low = split(own)
    near = jnp.where(lane < 2 * EDGE, beside, 0.0)
    near_high = near.astype(BF16).astype(F32)
    near_low = near - near_high
    near = near_high + shifted(near_low, 2 * EDGE) + shifted(near_high, 4 * EDGE)
    terms = jnp.concatenate([high, low, high, near.astype(BF16)], axis=1)
    for pair in range(0, count, 2):
        both = lax.dot_general(terms, col_band_ref[pair // 2], NN, preferred_element_type=F32)
        for k, b in enumerate(range(pair, min(pair + 2, count))):
            across_ref[b, at, :] = jnp.concatenate(split(both[:, k * LANES : (k + 1) * LANES]), axis=1)


def row_pass(starts, row_band_ref, across_ref, images_ref, pitch):
    count = across_ref.shape[0]
    _, size, width = row_band_ref.shape
    for b in range(count):
        sides = []
        for start in starts:
            across = across_ref[b, pl.ds(start, width // 3), :]
            sides.append(jnp.concatenate([across[:, :LANES], across[:, LANES:], across[:, :LANES]], axis=0))
        both = lax.dot_general(
            row_band_ref[b], jnp.concatenate(sides, axis=1), NN, preferred_element_type=F32
        )
        for k, start in enumerate(starts):
            images_ref[pl.ds(b * pitch + start, size), :] = both[:, k * LANES : (k + 1) * LANES]


def make_weight(srow_ref, scol_ref, cov_ref, root_ref, total):
    _, rows, cols = root_ref.shape
    stamps = srow_ref.shape[1]
    at = iota((cols, stamps), 0) - scol_ref[...]
    cols_in = jnp.where((at >= 0) & (at < S), cov_ref[...].astype(F32), 0.0).astype(BF16)
    at = iota((rows, stamps), 0) - srow_ref[...]
    rows_in = jnp.where((at >= 0) & (at < S), 1.0, 0.0).astype(BF16)
    root = jnp.sqrt(lax.dot_general(rows_in, cols_in, NT, preferred_element_type=F32))
    root_ref[0] = root
    root_ref[1] = root * xi_row(cols, total)
    root_ref[2] = root * (2.0 * iota((rows, 1), 0).astype(F32) / rows - 1.0)


def gram(starts, size, root_ref, images_ref, first_ref, second_ref, pitch):
    upper = iota((8, images_ref.shape[1]), 0) < 4

    def row(y):
        low, high, cross = (images_ref[pl.ds(k * pitch + y, 8, stride=pitch), :] for k in (0, 8, 4))
        plain, by_xi, by_eta = (jnp.broadcast_to(root_ref[k, pl.ds(y, 1), :], low.shape) for k in range(3))
        body = jnp.concatenate([low * plain, high * plain, low * by_xi, low * by_eta], axis=0)
        return body, jnp.where(upper, high, cross) * jnp.where(upper, by_xi, by_eta)

    def terms(start):
        body, rest = (jnp.concatenate(v, axis=1) for v in zip(*[row(start + j) for j in range(TURN)]))
        high, low = split(body)
        rest = jnp.concatenate([rest, rest - rest.astype(BF16).astype(F32)], axis=0).astype(BF16)
        short = jnp.concatenate([high, rest], axis=0)
        return short, jnp.concatenate([short, low], axis=0)

    first, second = first_ref[...], second_ref[...]
    step = size * len(starts) // 2
    near, far = starts[0], starts[0] + step if len(starts) == 1 else starts[1]
    for turn in range(0, step, TURN):
        short, whole = terms(near + turn)
        first = first + lax.dot_general(short, whole, NT, preferred_element_type=F32)
        short, whole = terms(far + turn)
        second = second + lax.dot_general(whole, short, NT, preferred_element_type=F32)
    first_ref[...], second_ref[...] = first, second


def combine(first_ref, second_ref):
    def pad(value, rows=SIDE):
        value = jnp.concatenate([value, jnp.zeros((value.shape[0], LANES - value.shape[1]), F32)], axis=1)
        if rows == value.shape[0]:
            return value
        return jnp.concatenate([value, jnp.zeros((rows - value.shape[0], LANES), F32)], axis=0)

    first, second = first_ref[:SIDE], second_ref[:, :SIDE]
    mixed = jnp.concatenate([first[:, DUAL:], first[:, SIDE:DUAL]], axis=1)
    mixed = mixed + jnp.concatenate([second[DUAL:], second[SIDE:DUAL]], axis=0)
    turned = jnp.transpose(pad(mixed, LANES))[:SIDE]
    return pad(first[:, :SIDE] + second[:SIDE]) + (pad(mixed) + turned)


def place(kind, b):
    if kind == 0:
        return b
    return (8 + 8 * kind + b) if b < 8 else (28 + 4 * kind + b - 8)


def solve(normal, count):
    side = SIDE
    row, col = iota((side, LANES), 0), iota((side, LANES), 1)
    unknowns = sorted([place(kind, b) for kind in range(3) for b in range(count)] + [count])

    def used(k):
        spare = [p for p in range(side) if p not in unknowns]
        keep = k < side
        for p in spare:
            keep = keep & (k != p)
        return keep

    rhs = normal[:, count + 1 : count + 2]
    system = jnp.where(used(row) & used(col), normal, 0.0) + ridge_weight * jnp.where(row == col, 1.0, 0.0)
    system = jnp.where((col == side) & used(row), rhs, system)
    scale = jnp.zeros((side, LANES), F32)
    for first in range(0, len(unknowns), BLOCK):
        block = unknowns[first : first + BLOCK]
        columns = [jnp.broadcast_to(system[:, p : p + 1], (side, LANES)) for p in block]
        for k, p in enumerate(block):
            column = columns[k]
            inverse = 1.0 / column[p : p + 1, :]
            scale = jnp.where(row == p, inverse, scale)
            factor = jnp.where(row == p, 0.0, column)
            for later in range(k + 1, len(block)):
                columns[later] = columns[later] - factor * (columns[later][p : p + 1, :] * inverse)
            system = system - factor * (system[p : p + 1, :] * inverse)
    return jnp.broadcast_to(system[:, side : side + 1], (side, LANES)) * scale


def apply(coefs, images_ref, science_ref, out_ref, pitch, count, total):
    _, rows, cols = science_ref.shape
    xi = xi_row(cols, total)
    wide = lambda k: jnp.broadcast_to(coefs[k : k + 1, :], (8, cols))
    flat = [wide(b) + wide(place(1, b)) * xi for b in range(count)]
    slope = [wide(place(2, b)) for b in range(count)]
    constant = wide(count)
    step = 4 if rows % 32 == 0 else 1

    def body(turn, carry):
        for k in range(step):
            start = pl.multiple_of((turn * step + k) * 8, 8)
            eta = 2.0 * (start + iota((8, cols), 0)).astype(F32) / rows - 1.0
            field = constant
            for b in range(count):
                field = field + images_ref[pl.ds(b * pitch + start, 8), :] * (flat[b] + slope[b] * eta)
            out_ref[0, pl.ds(start, 8), :] = science_ref[0, pl.ds(start, 8), :] - field
        return carry

    lax.fori_loop(0, rows // (8 * step), body, 0)


def remote(source, target, send, recv, epoch, tile):
    return pltpu.make_async_remote_copy(
        src_ref=source,
        dst_ref=target,
        send_sem=send,
        recv_sem=recv,
        device_id={"epoch": epoch, "tile": tile},
        device_id_type=pl.DeviceIdType.MESH,
    )


def kernel(total, top, pitch, template_in, science_in, rowp_in, colp_in, cov_in, srow_in, scol_in, out_ref,
           science_ref, rowp_ref, colp_ref, cov_ref, srow_ref, scol_ref,
           slots, pack, edges, across_ref, parts, mine, images_ref, root_ref, first_ref, second_ref, profile_ref,
           row_band_ref, col_band_ref, slot_send, slot_recv, edge_send, edge_recv,
           part_send, part_recv, load_sem, hello):
    count, taps = rowp_ref.shape
    _, rows, cols = science_ref.shape
    epochs, own_rows, _ = slots.shape
    tiles = parts.shape[0]
    size = row_band_ref.shape[1]
    epoch, tile = lax.axis_index("epoch"), lax.axis_index("tile")

    loads = [
        pltpu.make_async_copy(source, target, load_sem.at[k])
        for k, (source, target) in enumerate(
            [
                (template_in, slots.at[epoch]),
                (rowp_in, rowp_ref),
                (colp_in, colp_ref),
                (cov_in, cov_ref),
                (srow_in, srow_ref),
                (scol_in, scol_ref),
                (science_in, science_ref),
            ]
        )
    ]
    for load in loads:
        load.start()
    barrier = pltpu.get_barrier_semaphore()
    has_left, has_right = tile > 0, tile < tiles - 1

    def greet(semaphore, e, t):
        pl.semaphore_signal(semaphore, inc=1, device_id={"epoch": e, "tile": t}, device_id_type=pl.DeviceIdType.MESH)

    for t in range(1, tiles):
        greet(barrier, epoch, lax.rem(tile + t, tiles))

    def greet_above(target, carry):
        greet(barrier, target, tile)

        @pl.when(has_left)
        def _():
            greet(barrier, target, tile - 1)

        @pl.when(has_right)
        def _():
            greet(barrier, target, tile + 1)

        return carry

    lax.fori_loop(epoch + 1, epochs, greet_above, 0)
    loads[0].wait()
    flipped = jnp.transpose(slots[epoch])
    pack[0] = flipped[:EDGE]
    pack[1] = flipped[cols - EDGE :]
    around = 1 + has_left.astype(jnp.int32) + has_right.astype(jnp.int32)
    pl.semaphore_wait(barrier, tiles - 1 + epoch * around)

    def announce(target, carry):
        greet(hello.at[epoch], target, tile)
        return carry

    lax.fori_loop(0, epoch, announce, 0)

    def block_copy(target, source):
        return remote(slots.at[source], slots.at[source], slot_send.at[target], slot_recv.at[source], target, tile)

    def edge_copy(target, side, source):
        place = pl.ds((1 - side) * EDGE, EDGE)
        return remote(pack.at[side], edges.at[source, place], edge_send.at[side, target], edge_recv.at[1 - side, source],
                      target, tile + 2 * side - 1)

    def send(target, carry):
        for side, there in ((0, has_left), (1, has_right)):

            @pl.when(there)
            def _():
                edge_copy(target, side, epoch).start()

        @pl.when(target != epoch)
        def _():
            block_copy(target, epoch).start()

        return carry

    def send_up(target):
        @pl.when(target < epochs)
        def _():
            pl.semaphore_wait(hello.at[target], 1)
            send(target, 0)

    lax.fori_loop(0, epoch + 1, send, 0)

    for side, there in ((0, has_left), (1, has_right)):

        @pl.when(jnp.logical_not(there))
        def _():
            edges[:, side * EDGE : (side + 1) * EDGE, :] = jnp.zeros((epochs, EDGE, own_rows), F32)

    for load in loads[1:]:
        load.wait()
    make_bands(rowp_ref, colp_ref, profile_ref, row_band_ref, col_band_ref, top - taps // 2)
    high = across_ref.shape[1]
    send_up(epoch + 1)
    across_ref[:, :top, :] = jnp.zeros((count, top, 2 * cols), BF16)
    across_ref[:, top + rows :, :] = jnp.zeros((count, high - top - rows, 2 * cols), BF16)

    make_weight(srow_ref, scol_ref, cov_ref, root_ref, total)
    images_ref[pl.ds(count * pitch, rows), :] = jnp.ones((rows, cols), F32)
    images_ref[pl.ds((count + 1) * pitch, rows), :] = science_ref[0]
    for spare in range(count + 2, GROUP):
        images_ref[pl.ds(spare * pitch, rows), :] = jnp.zeros((rows, cols), F32)
    first_ref[...] = jnp.zeros_like(first_ref)
    second_ref[...] = jnp.zeros_like(second_ref)

    each = 2 * size // own_rows
    chunks = rows // (2 * size)
    middle = jnp.zeros((cols - 2 * EDGE, own_rows), F32)

    def columns(chunk):
        owns = [slots[chunk * each + k] for k in range(each)]
        sides = [jnp.transpose(jnp.concatenate([edges[chunk * each + k], middle], axis=0)) for k in range(each)]
        at = pl.ds(pl.multiple_of(top + chunk * 2 * size, 16), 2 * size)
        column_pass(jnp.concatenate(owns, axis=0), jnp.concatenate(sides, axis=0), at, col_band_ref, across_ref)

    def work(units):
        starts = [pl.multiple_of(unit * size, 16) for unit in units]
        row_pass(starts, row_band_ref, across_ref, images_ref, pitch)
        gram(starts, size, root_ref, images_ref, first_ref, second_ref, pitch)

    def arrive(source):
        @pl.when(source != epoch)
        def _():
            block_copy(epoch, source).wait_recv()

        for side, there in ((0, has_left), (1, has_right)):

            @pl.when(there)
            def _():
                edge_copy(epoch, 1 - side, source).wait_recv()

    def step(d, carry):
        @pl.when(d > 0)
        def _():
            send_up(epoch + d + 1)

        def side(k, carry):
            right = (k + (2 * epoch < epochs).astype(jnp.int32)) % 2 == 0
            source = epoch + jnp.where(right, d, -d)
            valid = (source >= 0) & (source < epochs) & ((d > 0) | (k == 0))

            @pl.when(valid)
            def _():
                arrive(source)

            if each == 1:

                @pl.when(valid)
                def _():
                    columns(source)

                far = (epoch + d >= epochs - 1) & (epoch - d <= 0)
                other = epoch + jnp.where(right, -d, d)
                done = far & ((k == 1) | (other < 0) | (other >= epochs)) & (d > 0)
                lone = (epoch == 0) | (epoch == epochs - 1)

                def ready(turn, carry):
                    chunk = jnp.where(turn == 0, source + jnp.where(right, 0, 1), 0)
                    work((jnp.where(turn == 0, 2 * chunk - 1, 0), jnp.where(turn == 0, 2 * chunk, 2 * chunks - 1)))
                    return carry

                pairs = (d > 0).astype(jnp.int32) + (done & jnp.logical_not(lone)).astype(jnp.int32)
                lax.fori_loop(0, jnp.where(valid, pairs, 0), ready, 0)

                def margin(turn, carry):
                    work((jnp.where((turn == 0) & (source == 0), 0, 2 * chunks - 1),))
                    return carry

                margins = (source == 0).astype(jnp.int32) + (source == epochs - 1).astype(jnp.int32)
                lax.fori_loop(0, jnp.where(valid & lone, margins, 0), margin, 0)
            return carry

        lax.fori_loop(0, 2, side, 0)
        return carry

    lax.fori_loop(0, epochs, step, 0)
    if each > 1:

        def fresh_chunk(chunk, carry):
            columns(chunk)
            return carry

        def ready_chunk(chunk, carry):
            work((2 * chunk - 1, 2 * chunk))
            return carry

        def margin_unit(turn, carry):
            work((turn * (2 * chunks - 1),))
            return carry

        lax.fori_loop(0, chunks, fresh_chunk, 0)
        lax.fori_loop(1, chunks, ready_chunk, 0)
        lax.fori_loop(0, 2, margin_unit, 0)

    normal = combine(first_ref, second_ref)
    under = jnp.concatenate([normal[FOLD:], jnp.zeros((2 * FOLD - SIDE, LANES), F32)], axis=0)
    normal = normal[:FOLD] + shifted(under, HALF)
    mine[...] = normal

    def part_copy(t, source):
        return remote(mine, parts.at[source], part_send.at[t], part_recv.at[source],
                      epoch, lax.rem(tile + t, tiles))

    for t in range(1, tiles):
        part_copy(t, tile).start()
    for t in range(1, tiles):
        source = lax.rem(tile + tiles - t, tiles)
        part_copy(t, source).wait_recv()
        normal = normal + parts[source]
    for t in range(1, tiles):
        part_copy(t, tile).wait_send()

    def sent(target, carry):
        @pl.when(target != epoch)
        def _():
            block_copy(target, epoch).wait_send()

        for side, there in ((0, has_left), (1, has_right)):

            @pl.when(there)
            def _():
                edge_copy(target, side, epoch).wait_send()

        return carry

    lax.fori_loop(0, epochs, sent, 0)
    lane = iota((1, LANES), 1)
    normal = jnp.concatenate(
        [jnp.where(lane < HALF, normal, 0.0), jnp.where(lane < HALF, shifted(normal, HALF), 0.0)[: SIDE - FOLD]], axis=0
    )
    coefs = solve(normal, count)
    apply(coefs, images_ref, science_ref, out_ref, pitch, count, total)


def local(template, science, row_profiles, col_profiles, coverage, stamp_rows, stamp_cols):
    count, taps = row_profiles.shape
    rows, cols = science.shape[1:]
    own_rows = template.shape[0]
    tiles, epochs = lax.axis_size("tile"), lax.axis_size("epoch")
    top = -(-(taps // 2) // 16) * 16
    size = unit_rows(rows, own_rows, top)
    pitch = rows + 4
    vmem = pl.BlockSpec(memory_space=pltpu.VMEM)
    dma = pltpu.SemaphoreType.DMA
    operands = (
        template,
        science,
        row_profiles,
        col_profiles,
        coverage,
        stamp_rows.reshape(1, -1),
        stamp_cols.reshape(1, -1),
    )
    return pl.pallas_call(
        functools.partial(kernel, cols * tiles, top, pitch),
        out_shape=jax.ShapeDtypeStruct(science.shape, F32),
        in_specs=[pl.BlockSpec(memory_space=pl.ANY)] * 7,
        out_specs=vmem,
        scratch_shapes=[
            pltpu.VMEM(science.shape, F32),
            pltpu.VMEM(row_profiles.shape, F32),
            pltpu.VMEM(col_profiles.shape, F32),
            pltpu.VMEM(coverage.shape, jnp.int32),
            pltpu.VMEM((1, stamp_rows.shape[0]), jnp.int32),
            pltpu.VMEM((1, stamp_cols.shape[0]), jnp.int32),
            pltpu.VMEM((epochs, own_rows, cols), F32),
            pltpu.VMEM((2, EDGE, own_rows), F32),
            pltpu.VMEM((epochs, 2 * EDGE, own_rows), F32),
            pltpu.VMEM((count, rows + 2 * top, 2 * cols), BF16),
            pltpu.VMEM((tiles, FOLD, LANES), F32),
            pltpu.VMEM((FOLD, LANES), F32),
            pltpu.VMEM((GROUP * pitch, cols), F32),
            pltpu.VMEM((3, rows, cols), F32),
            pltpu.VMEM((DUAL, BOTH), F32),
            pltpu.VMEM((BOTH, DUAL), F32),
            pltpu.VMEM((3, GROUP, 2 * LANES), F32),
            pltpu.VMEM((count, size, 3 * (size + 2 * top)), BF16),
            pltpu.VMEM((-(-count // 2), 4 * LANES, 2 * LANES), BF16),
            dma((epochs,)),
            dma((epochs,)),
            dma((2, epochs)),
            dma((2, epochs)),
            dma((tiles,)),
            dma((tiles,)),
            dma((7,)),
            pltpu.SemaphoreType.REGULAR((epochs,)),
        ],
        compiler_params=pltpu.CompilerParams(
            collective_id=0, has_side_effects=True, vmem_limit_bytes=48 * 2**20
        ),
    )(*(pltpu.with_memory_space_constraint(operand, pltpu.HBM) for operand in operands))


def solution(mesh):
    in_specs = (
        P(("patch", "epoch"), "tile"),
        P(("patch", "epoch"), None, "tile"),
        P(),
        P(),
        P(("patch", "epoch"), "tile"),
        P(("patch", "tile")),
        P(("patch", "tile")),
    )
    out_specs = P(("patch", "epoch"), None, "tile")
    return jax.shard_map(local, mesh=mesh, in_specs=in_specs, out_specs=out_specs, check_vma=False)
```

```python
import functools

import jax
import jax.numpy as jnp
from jax import lax
from jax.experimental import pallas as pl
from jax.experimental.pallas import tpu as pltpu
from jax.sharding import PartitionSpec as P

S = 32
GROUP = 16
EDGE = 16
LANES = 128
HALF = LANES // 2
BLOCK = 13
SIDE = 40
TURN = 8
FOLD = 24
DUAL = 48
BOTH = 80
ridge_weight = 1.0
F32 = jnp.float32
BF16 = jnp.bfloat16
NT = (((1,), (1,)), ((), ()))
NN = (((1,), (0,)), ((), ()))


def split(value):
    high = value.astype(BF16)
    return high, (value - high.astype(F32)).astype(BF16)


def iota(shape, axis):
    return lax.broadcasted_iota(jnp.int32, shape, axis)


def shifted(value, turn):
    turn %= value.shape[1]
    return pltpu.roll(value, turn, 1) if turn else value


def toeplitz(profile_row, rows, turn=0):
    width = profile_row.shape[1]
    base = pltpu.roll(jnp.broadcast_to(profile_row, (8, width)), 0, 1, stride=1, stride_axis=0)
    return jnp.concatenate([shifted(base, turn + first) for first in range(0, rows, 8)], axis=0)


def xi_row(cols, total):
    start = lax.axis_index("tile") * cols
    return 2.0 * (start + iota((1, cols), 1)).astype(F32) / total - 1.0


def unit_rows(rows, own, top):
    sizes = [r for r in range(16, 2 * LANES // 3 - 2 * top + 1, 16) if rows % (2 * r) == 0 and 2 * r % own == 0]
    return max(sizes)


def make_bands(rowp_ref, colp_ref, profile_ref, row_band_ref, col_band_ref, shift):
    count, taps = rowp_ref.shape
    half = taps // 2
    profile_ref[...] = jnp.zeros_like(profile_ref)
    high, low = (part.astype(F32) for part in split(rowp_ref[...]))
    _, size, width = row_band_ref.shape
    for k, part in enumerate((high, high, low)):
        at = k * (width // 3) + shift
        profile_ref[0, :count, at : at + taps] = part
    flip = jnp.where(iota((taps, taps), 0) + iota((taps, taps), 1) == taps - 1, 1.0, 0.0).astype(BF16)
    for k, part in enumerate(split(colp_ref[...])):
        profile_ref[1 + k, :count, :taps] = lax.dot_general(part, flip, NN, preferred_element_type=F32)
    gap = jnp.zeros((LANES - 6 * EDGE, LANES), BF16)
    for b in range(count):
        row_band_ref[b] = toeplitz(profile_ref[0, b : b + 1, :], size)[:, :width].astype(BF16)
        parts = []
        for k in (1, 2):
            tall = toeplitz(profile_ref[k, b : b + 1, :], LANES + 2 * EDGE, -half - EDGE)[:, :LANES].astype(BF16)
            beside = jnp.concatenate([tall[:EDGE], tall[EDGE + LANES :]], axis=0)
            parts.append((tall[EDGE : EDGE + LANES], beside))
        (high, near_high), (low, near_low) = parts
        at = pl.ds((b % 2) * LANES, LANES)
        column = jnp.concatenate([high, high, low, near_high, near_high, near_low, gap], axis=0)
        col_band_ref[b // 2, :, at] = column


def column_pass(own, beside, at, col_band_ref, across_ref):
    count = across_ref.shape[0]
    lane = iota((1, LANES), 1)
    high, low = split(own)
    near = jnp.where(lane < 2 * EDGE, beside, 0.0)
    near_high = near.astype(BF16).astype(F32)
    near_low = near - near_high
    near = near_high + shifted(near_low, 2 * EDGE) + shifted(near_high, 4 * EDGE)
    terms = jnp.concatenate([high, low, high, near.astype(BF16)], axis=1)
    for pair in range(0, count, 2):
        both = lax.dot_general(terms, col_band_ref[pair // 2], NN, preferred_element_type=F32)
        for k, b in enumerate(range(pair, min(pair + 2, count))):
            across_ref[b, at, :] = jnp.concatenate(split(both[:, k * LANES : (k + 1) * LANES]), axis=1)


def row_pass(starts, row_band_ref, across_ref, images_ref, pitch):
    count = across_ref.shape[0]
    _, size, width = row_band_ref.shape
    for b in range(count):
        sides = []
        for start in starts:
            across = across_ref[b, pl.ds(start, width // 3), :]
            sides.append(jnp.concatenate([across[:, :LANES], across[:, LANES:], across[:, :LANES]], axis=0))
        both = lax.dot_general(
            row_band_ref[b], jnp.concatenate(sides, axis=1), NN, preferred_element_type=F32
        )
        for k, start in enumerate(starts):
            images_ref[pl.ds(b * pitch + start, size), :] = both[:, k * LANES : (k + 1) * LANES]


def make_weight(srow_ref, scol_ref, cov_ref, root_ref, total):
    _, rows, cols = root_ref.shape
    stamps = srow_ref.shape[1]
    at = iota((cols, stamps), 0) - scol_ref[...]
    cols_in = jnp.where((at >= 0) & (at < S), cov_ref[...].astype(F32), 0.0).astype(BF16)
    at = iota((rows, stamps), 0) - srow_ref[...]
    rows_in = jnp.where((at >= 0) & (at < S), 1.0, 0.0).astype(BF16)
    root = jnp.sqrt(lax.dot_general(rows_in, cols_in, NT, preferred_element_type=F32))
    root_ref[0] = root
    root_ref[1] = root * xi_row(cols, total)
    root_ref[2] = root * (2.0 * iota((rows, 1), 0).astype(F32) / rows - 1.0)


def gram(starts, size, root_ref, images_ref, first_ref, second_ref, pitch):
    upper = iota((8, images_ref.shape[1]), 0) < 4

    def row(y):
        low, high, cross = (images_ref[pl.ds(k * pitch + y, 8, stride=pitch), :] for k in (0, 8, 4))
        plain, by_xi, by_eta = (jnp.broadcast_to(root_ref[k, pl.ds(y, 1), :], low.shape) for k in range(3))
        body = jnp.concatenate([low * plain, high * plain, low * by_xi, low * by_eta], axis=0)
        return body, jnp.where(upper, high, cross) * jnp.where(upper, by_xi, by_eta)

    def terms(start):
        body, rest = (jnp.concatenate(v, axis=1) for v in zip(*[row(start + j) for j in range(TURN)]))
        high, low = split(body)
        rest = jnp.concatenate([rest, rest - rest.astype(BF16).astype(F32)], axis=0).astype(BF16)
        short = jnp.concatenate([high, rest], axis=0)
        return short, jnp.concatenate([short, low], axis=0)

    first, second = first_ref[...], second_ref[...]
    step = size * len(starts) // 2
    near, far = starts[0], starts[0] + step if len(starts) == 1 else starts[1]
    for turn in range(0, step, TURN):
        short, whole = terms(near + turn)
        first = first + lax.dot_general(short, whole, NT, preferred_element_type=F32)
        short, whole = terms(far + turn)
        second = second + lax.dot_general(whole, short, NT, preferred_element_type=F32)
    first_ref[...], second_ref[...] = first, second


def combine(first_ref, second_ref):
    def pad(value, rows=SIDE):
        value = jnp.concatenate([value, jnp.zeros((value.shape[0], LANES - value.shape[1]), F32)], axis=1)
        if rows == value.shape[0]:
            return value
        return jnp.concatenate([value, jnp.zeros((rows - value.shape[0], LANES), F32)], axis=0)

    first, second = first_ref[:SIDE], second_ref[:, :SIDE]
    mixed = jnp.concatenate([first[:, DUAL:], first[:, SIDE:DUAL]], axis=1)
    mixed = mixed + jnp.concatenate([second[DUAL:], second[SIDE:DUAL]], axis=0)
    turned = jnp.transpose(pad(mixed, LANES))[:SIDE]
    return pad(first[:, :SIDE] + second[:SIDE]) + (pad(mixed) + turned)


def place(kind, b):
    if kind == 0:
        return b
    return (8 + 8 * kind + b) if b < 8 else (28 + 4 * kind + b - 8)


def solve(normal, count):
    side = SIDE
    row, col = iota((side, LANES), 0), iota((side, LANES), 1)
    unknowns = sorted([place(kind, b) for kind in range(3) for b in range(count)] + [count])

    def used(k):
        spare = [p for p in range(side) if p not in unknowns]
        keep = k < side
        for p in spare:
            keep = keep & (k != p)
        return keep

    rhs = normal[:, count + 1 : count + 2]
    system = jnp.where(used(row) & used(col), normal, 0.0) + ridge_weight * jnp.where(row == col, 1.0, 0.0)
    system = jnp.where((col == side) & used(row), rhs, system)
    scale = jnp.zeros((side, LANES), F32)
    for first in range(0, len(unknowns), BLOCK):
        block = unknowns[first : first + BLOCK]
        columns = [jnp.broadcast_to(system[:, p : p + 1], (side, LANES)) for p in block]
        for k, p in enumerate(block):
            column = columns[k]
            inverse = 1.0 / column[p : p + 1, :]
            scale = jnp.where(row == p, inverse, scale)
            factor = jnp.where(row == p, 0.0, column)
            for later in range(k + 1, len(block)):
                columns[later] = columns[later] - factor * (columns[later][p : p + 1, :] * inverse)
            system = system - factor * (system[p : p + 1, :] * inverse)
    return jnp.broadcast_to(system[:, side : side + 1], (side, LANES)) * scale


def apply(coefs, images_ref, science_ref, out_ref, pitch, count, total):
    _, rows, cols = science_ref.shape
    xi = xi_row(cols, total)
    wide = lambda k: jnp.broadcast_to(coefs[k : k + 1, :], (8, cols))
    flat = [wide(b) + wide(place(1, b)) * xi for b in range(count)]
    slope = [wide(place(2, b)) for b in range(count)]
    constant = wide(count)
    step = 4 if rows % 32 == 0 else 1

    def body(turn, carry):
        for k in range(step):
            start = pl.multiple_of((turn * step + k) * 8, 8)
            eta = 2.0 * (start + iota((8, cols), 0)).astype(F32) / rows - 1.0
            field = constant
            for b in range(count):
                field = field + images_ref[pl.ds(b * pitch + start, 8), :] * (flat[b] + slope[b] * eta)
            out_ref[0, pl.ds(start, 8), :] = science_ref[0, pl.ds(start, 8), :] - field
        return carry

    lax.fori_loop(0, rows // (8 * step), body, 0)


def remote(source, target, send, recv, epoch, tile):
    return pltpu.make_async_remote_copy(
        src_ref=source,
        dst_ref=target,
        send_sem=send,
        recv_sem=recv,
        device_id={"epoch": epoch, "tile": tile},
        device_id_type=pl.DeviceIdType.MESH,
    )


def kernel(total, top, pitch, template_in, science_in, rowp_in, colp_in, cov_in, srow_in, scol_in, out_ref,
           science_ref, rowp_ref, colp_ref, cov_ref, srow_ref, scol_ref,
           slots, pack, edges, across_ref, parts, mine, images_ref, root_ref, first_ref, second_ref, profile_ref,
           row_band_ref, col_band_ref, slot_send, slot_recv, edge_send, edge_recv,
           part_send, part_recv, load_sem, hello):
    count, taps = rowp_ref.shape
    _, rows, cols = science_ref.shape
    epochs, own_rows, _ = slots.shape
    tiles = parts.shape[0]
    size = row_band_ref.shape[1]
    epoch, tile = lax.axis_index("epoch"), lax.axis_index("tile")

    loads = [
        pltpu.make_async_copy(source, target, load_sem.at[k])
        for k, (source, target) in enumerate(
            [
                (template_in, slots.at[epoch]),
                (rowp_in, rowp_ref),
                (colp_in, colp_ref),
                (cov_in, cov_ref),
                (srow_in, srow_ref),
                (scol_in, scol_ref),
                (science_in, science_ref),
            ]
        )
    ]
    for load in loads:
        load.start()
    barrier = pltpu.get_barrier_semaphore()
    has_left, has_right = tile > 0, tile < tiles - 1

    def greet(semaphore, e, t):
        pl.semaphore_signal(semaphore, inc=1, device_id={"epoch": e, "tile": t}, device_id_type=pl.DeviceIdType.MESH)

    for t in range(1, tiles):
        greet(barrier, epoch, lax.rem(tile + t, tiles))

    def greet_above(target, carry):
        greet(barrier, target, tile)

        @pl.when(has_left)
        def _():
            greet(barrier, target, tile - 1)

        @pl.when(has_right)
        def _():
            greet(barrier, target, tile + 1)

        return carry

    lax.fori_loop(epoch + 1, epochs, greet_above, 0)
    loads[0].wait()
    flipped = jnp.transpose(slots[epoch])
    pack[0] = flipped[:EDGE]
    pack[1] = flipped[cols - EDGE :]
    around = 1 + has_left.astype(jnp.int32) + has_right.astype(jnp.int32)
    pl.semaphore_wait(barrier, tiles - 1 + epoch * around)

    def announce(target, carry):
        greet(hello.at[epoch], target, tile)
        return carry

    lax.fori_loop(0, epoch, announce, 0)

    def block_copy(target, source):
        return remote(slots.at[source], slots.at[source], slot_send.at[target], slot_recv.at[source], target, tile)

    def edge_copy(target, side, source):
        place = pl.ds((1 - side) * EDGE, EDGE)
        return remote(pack.at[side], edges.at[source, place], edge_send.at[side, target], edge_recv.at[1 - side, source],
                      target, tile + 2 * side - 1)

    def send(target, carry):
        @pl.when(target != epoch)
        def _():
            block_copy(target, epoch).start()

        for side, there in ((0, has_left), (1, has_right)):

            @pl.when(there)
            def _():
                edge_copy(target, side, epoch).start()

        return carry

    def send_up(target):
        @pl.when(target < epochs)
        def _():
            pl.semaphore_wait(hello.at[target], 1)
            send(target, 0)

    shift = jnp.where(epoch == epochs - 1, jnp.maximum(epochs - 2, 0), 0)
    lax.fori_loop(0, epoch + 1, lambda k, carry: send(lax.rem(k + shift, epoch + 1), carry), 0)

    for side, there in ((0, has_left), (1, has_right)):

        @pl.when(jnp.logical_not(there))
        def _():
            edges[:, side * EDGE : (side + 1) * EDGE, :] = jnp.zeros((epochs, EDGE, own_rows), F32)

    for load in loads[1:]:
        load.wait()
    make_bands(rowp_ref, colp_ref, profile_ref, row_band_ref, col_band_ref, top - taps // 2)
    high = across_ref.shape[1]
    send_up(epoch + 1)
    across_ref[:, :top, :] = jnp.zeros((count, top, 2 * cols), BF16)
    across_ref[:, top + rows :, :] = jnp.zeros((count, high - top - rows, 2 * cols), BF16)

    make_weight(srow_ref, scol_ref, cov_ref, root_ref, total)
    images_ref[pl.ds(count * pitch, rows), :] = jnp.ones((rows, cols), F32)
    images_ref[pl.ds((count + 1) * pitch, rows), :] = science_ref[0]
    for spare in range(count + 2, GROUP):
        images_ref[pl.ds(spare * pitch, rows), :] = jnp.zeros((rows, cols), F32)
    first_ref[...] = jnp.zeros_like(first_ref)
    second_ref[...] = jnp.zeros_like(second_ref)

    each = 2 * size // own_rows
    chunks = rows // (2 * size)
    middle = jnp.zeros((cols - 2 * EDGE, own_rows), F32)

    def columns(chunk):
        owns = [slots[chunk * each + k] for k in range(each)]
        sides = [jnp.transpose(jnp.concatenate([edges[chunk * each + k], middle], axis=0)) for k in range(each)]
        at = pl.ds(pl.multiple_of(top + chunk * 2 * size, 16), 2 * size)
        column_pass(jnp.concatenate(owns, axis=0), jnp.concatenate(sides, axis=0), at, col_band_ref, across_ref)

    def work(units):
        starts = [pl.multiple_of(unit * size, 16) for unit in units]
        row_pass(starts, row_band_ref, across_ref, images_ref, pitch)
        gram(starts, size, root_ref, images_ref, first_ref, second_ref, pitch)

    def arrive(source):
        @pl.when(source != epoch)
        def _():
            block_copy(epoch, source).wait_recv()

        for side, there in ((0, has_left), (1, has_right)):

            @pl.when(there)
            def _():
                edge_copy(epoch, 1 - side, source).wait_recv()

    def step(d, carry):
        @pl.when(d > 0)
        def _():
            send_up(epoch + d + 1)

        def side(k, carry):
            right = (k + (2 * epoch < epochs).astype(jnp.int32)) % 2 == 0
            source = epoch + jnp.where(right, d, -d)
            valid = (source >= 0) & (source < epochs) & ((d > 0) | (k == 0))

            @pl.when(valid)
            def _():
                arrive(source)

            if each == 1:

                @pl.when(valid)
                def _():
                    columns(source)

                far = (epoch + d >= epochs - 1) & (epoch - d <= 0)
                other = epoch + jnp.where(right, -d, d)
                done = far & ((k == 1) | (other < 0) | (other >= epochs)) & (d > 0)
                lone = (epoch == 0) | (epoch == epochs - 1)

                def ready(turn, carry):
                    chunk = jnp.where(turn == 0, source + jnp.where(right, 0, 1), 0)
                    work((jnp.where(turn == 0, 2 * chunk - 1, 0), jnp.where(turn == 0, 2 * chunk, 2 * chunks - 1)))
                    return carry

                pairs = (d > 0).astype(jnp.int32) + (done & jnp.logical_not(lone)).astype(jnp.int32)
                lax.fori_loop(0, jnp.where(valid, pairs, 0), ready, 0)

                def margin(turn, carry):
                    work((jnp.where((turn == 0) & (source == 0), 0, 2 * chunks - 1),))
                    return carry

                margins = (source == 0).astype(jnp.int32) + (source == epochs - 1).astype(jnp.int32)
                lax.fori_loop(0, jnp.where(valid & lone, margins, 0), margin, 0)
            return carry

        lax.fori_loop(0, 2, side, 0)
        return carry

    lax.fori_loop(0, epochs, step, 0)
    if each > 1:

        def fresh_chunk(chunk, carry):
            columns(chunk)
            return carry

        def ready_chunk(chunk, carry):
            work((2 * chunk - 1, 2 * chunk))
            return carry

        def margin_unit(turn, carry):
            work((turn * (2 * chunks - 1),))
            return carry

        lax.fori_loop(0, chunks, fresh_chunk, 0)
        lax.fori_loop(1, chunks, ready_chunk, 0)
        lax.fori_loop(0, 2, margin_unit, 0)

    normal = combine(first_ref, second_ref)
    under = jnp.concatenate([normal[FOLD:], jnp.zeros((2 * FOLD - SIDE, LANES), F32)], axis=0)
    normal = normal[:FOLD] + shifted(under, HALF)
    mine[...] = normal

    def part_copy(t, source):
        return remote(mine, parts.at[source], part_send.at[t], part_recv.at[source],
                      epoch, lax.rem(tile + t, tiles))

    for t in range(1, tiles):
        part_copy(t, tile).start()
    for t in range(1, tiles):
        source = lax.rem(tile + tiles - t, tiles)
        part_copy(t, source).wait_recv()
        normal = normal + parts[source]


    lane = iota((1, LANES), 1)
    normal = jnp.concatenate(
        [jnp.where(lane < HALF, normal, 0.0), jnp.where(lane < HALF, shifted(normal, HALF), 0.0)[: SIDE - FOLD]], axis=0
    )
    coefs = solve(normal, count)
    apply(coefs, images_ref, science_ref, out_ref, pitch, count, total)

    for t in range(1, tiles):
        part_copy(t, tile).wait_send()

    def sent(target, carry):
        @pl.when(target != epoch)
        def _():
            block_copy(target, epoch).wait_send()

        for side, there in ((0, has_left), (1, has_right)):

            @pl.when(there)
            def _():
                edge_copy(target, side, epoch).wait_send()

        return carry

    lax.fori_loop(0, epochs, sent, 0)


def local(template, science, row_profiles, col_profiles, coverage, stamp_rows, stamp_cols):
    count, taps = row_profiles.shape
    rows, cols = science.shape[1:]
    own_rows = template.shape[0]
    tiles, epochs = lax.axis_size("tile"), lax.axis_size("epoch")
    top = -(-(taps // 2) // 16) * 16
    size = unit_rows(rows, own_rows, top)
    pitch = rows + 4
    vmem = pl.BlockSpec(memory_space=pltpu.VMEM)
    dma = pltpu.SemaphoreType.DMA
    operands = (
        template,
        science,
        row_profiles,
        col_profiles,
        coverage,
        stamp_rows.reshape(1, -1),
        stamp_cols.reshape(1, -1),
    )
    return pl.pallas_call(
        functools.partial(kernel, cols * tiles, top, pitch),
        out_shape=jax.ShapeDtypeStruct(science.shape, F32),
        in_specs=[pl.BlockSpec(memory_space=pl.ANY)] * 7,
        out_specs=vmem,
        scratch_shapes=[
            pltpu.VMEM(science.shape, F32),
            pltpu.VMEM(row_profiles.shape, F32),
            pltpu.VMEM(col_profiles.shape, F32),
            pltpu.VMEM(coverage.shape, jnp.int32),
            pltpu.VMEM((1, stamp_rows.shape[0]), jnp.int32),
            pltpu.VMEM((1, stamp_cols.shape[0]), jnp.int32),
            pltpu.VMEM((epochs, own_rows, cols), F32),
            pltpu.VMEM((2, EDGE, own_rows), F32),
            pltpu.VMEM((epochs, 2 * EDGE, own_rows), F32),
            pltpu.VMEM((count, rows + 2 * top, 2 * cols), BF16),
            pltpu.VMEM((tiles, FOLD, LANES), F32),
            pltpu.VMEM((FOLD, LANES), F32),
            pltpu.VMEM((GROUP * pitch, cols), F32),
            pltpu.VMEM((3, rows, cols), F32),
            pltpu.VMEM((DUAL, BOTH), F32),
            pltpu.VMEM((BOTH, DUAL), F32),
            pltpu.VMEM((3, GROUP, 2 * LANES), F32),
            pltpu.VMEM((count, size, 3 * (size + 2 * top)), BF16),
            pltpu.VMEM((-(-count // 2), 4 * LANES, 2 * LANES), BF16),
            dma((epochs,)),
            dma((epochs,)),
            dma((2, epochs)),
            dma((2, epochs)),
            dma((tiles,)),
            dma((tiles,)),
            dma((7,)),
            pltpu.SemaphoreType.REGULAR((epochs,)),
        ],
        compiler_params=pltpu.CompilerParams(
            collective_id=0, has_side_effects=True, vmem_limit_bytes=48 * 2**20
        ),
    )(*(pltpu.with_memory_space_constraint(operand, pltpu.HBM) for operand in operands))


def solution(mesh):
    in_specs = (
        P(("patch", "epoch"), "tile"),
        P(("patch", "epoch"), None, "tile"),
        P(),
        P(),
        P(("patch", "epoch"), "tile"),
        P(("patch", "tile")),
        P(("patch", "tile")),
    )
    out_specs = P(("patch", "epoch"), None, "tile")
    return jax.shard_map(local, mesh=mesh, in_specs=in_specs, out_specs=out_specs, check_vma=False)
```

```python
import functools

import jax
import jax.numpy as jnp
from jax import lax
from jax.experimental import pallas as pl
from jax.experimental.pallas import tpu as pltpu
from jax.sharding import PartitionSpec as P

S = 32
GROUP = 16
EDGE = 16
LANES = 128
HALF = LANES // 2
BLOCK = 13
SIDE = 40
TURN = 8
FOLD = 24
DUAL = 48
BOTH = 80
ridge_weight = 1.0
F32 = jnp.float32
BF16 = jnp.bfloat16
NT = (((1,), (1,)), ((), ()))
NN = (((1,), (0,)), ((), ()))


def split(value):
    high = value.astype(BF16)
    return high, (value - high.astype(F32)).astype(BF16)


def iota(shape, axis):
    return lax.broadcasted_iota(jnp.int32, shape, axis)


def shifted(value, turn):
    turn %= value.shape[1]
    return pltpu.roll(value, turn, 1) if turn else value


def toeplitz(profile_row, rows, turn=0):
    width = profile_row.shape[1]
    base = pltpu.roll(jnp.broadcast_to(profile_row, (8, width)), 0, 1, stride=1, stride_axis=0)
    return jnp.concatenate([shifted(base, turn + first) for first in range(0, rows, 8)], axis=0)


def xi_row(cols, total):
    start = lax.axis_index("tile") * cols
    return 2.0 * (start + iota((1, cols), 1)).astype(F32) / total - 1.0


def unit_rows(rows, own, top):
    sizes = [r for r in range(16, 2 * LANES // 3 - 2 * top + 1, 16) if rows % (2 * r) == 0 and 2 * r % own == 0]
    return max(sizes)


def make_bands(rowp_ref, colp_ref, profile_ref, row_band_ref, col_band_ref, shift):
    count, taps = rowp_ref.shape
    half = taps // 2
    profile_ref[...] = jnp.zeros_like(profile_ref)
    high, low = (part.astype(F32) for part in split(rowp_ref[...]))
    _, size, width = row_band_ref.shape
    for k, part in enumerate((high, high, low)):
        at = k * (width // 3) + shift
        profile_ref[0, :count, at : at + taps] = part
    flip = jnp.where(iota((taps, taps), 0) + iota((taps, taps), 1) == taps - 1, 1.0, 0.0).astype(BF16)
    for k, part in enumerate(split(colp_ref[...])):
        profile_ref[1 + k, :count, :taps] = lax.dot_general(part, flip, NN, preferred_element_type=F32)
    gap = jnp.zeros((LANES - 6 * EDGE, LANES), BF16)
    for b in range(count):
        row_band_ref[b] = toeplitz(profile_ref[0, b : b + 1, :], size)[:, :width].astype(BF16)
        parts = []
        for k in (1, 2):
            tall = toeplitz(profile_ref[k, b : b + 1, :], LANES + 2 * EDGE, -half - EDGE)[:, :LANES].astype(BF16)
            beside = jnp.concatenate([tall[:EDGE], tall[EDGE + LANES :]], axis=0)
            parts.append((tall[EDGE : EDGE + LANES], beside))
        (high, near_high), (low, near_low) = parts
        at = pl.ds((b % 2) * LANES, LANES)
        column = jnp.concatenate([high, high, low, near_high, near_high, near_low, gap], axis=0)
        col_band_ref[b // 2, :, at] = column


def column_pass(own, beside, at, col_band_ref, across_ref):
    count = across_ref.shape[0]
    lane = iota((1, LANES), 1)
    high, low = split(own)
    near = jnp.where(lane < 2 * EDGE, beside, 0.0)
    near_high = near.astype(BF16).astype(F32)
    near_low = near - near_high
    near = near_high + shifted(near_low, 2 * EDGE) + shifted(near_high, 4 * EDGE)
    terms = jnp.concatenate([high, low, high, near.astype(BF16)], axis=1)
    for pair in range(0, count, 2):
        both = lax.dot_general(terms, col_band_ref[pair // 2], NN, preferred_element_type=F32)
        for k, b in enumerate(range(pair, min(pair + 2, count))):
            across_ref[b, at, :] = jnp.concatenate(split(both[:, k * LANES : (k + 1) * LANES]), axis=1)


def row_pass(starts, row_band_ref, across_ref, images_ref, pitch):
    count = across_ref.shape[0]
    _, size, width = row_band_ref.shape
    for b in range(count):
        sides = []
        for start in starts:
            across = across_ref[b, pl.ds(start, width // 3), :]
            sides.append(jnp.concatenate([across[:, :LANES], across[:, LANES:], across[:, :LANES]], axis=0))
        both = lax.dot_general(
            row_band_ref[b], jnp.concatenate(sides, axis=1), NN, preferred_element_type=F32
        )
        for k, start in enumerate(starts):
            images_ref[pl.ds(b * pitch + start, size), :] = both[:, k * LANES : (k + 1) * LANES]


def make_weight(srow_ref, scol_ref, cov_ref, root_ref, total):
    _, rows, cols = root_ref.shape
    stamps = srow_ref.shape[1]
    at = iota((cols, stamps), 0) - scol_ref[...]
    cols_in = jnp.where((at >= 0) & (at < S), cov_ref[...].astype(F32), 0.0).astype(BF16)
    at = iota((rows, stamps), 0) - srow_ref[...]
    rows_in = jnp.where((at >= 0) & (at < S), 1.0, 0.0).astype(BF16)
    root = jnp.sqrt(lax.dot_general(rows_in, cols_in, NT, preferred_element_type=F32))
    root_ref[0] = root
    root_ref[1] = root * xi_row(cols, total)
    root_ref[2] = root * (2.0 * iota((rows, 1), 0).astype(F32) / rows - 1.0)


def gram(starts, size, root_ref, images_ref, first_ref, second_ref, pitch):
    upper = iota((8, images_ref.shape[1]), 0) < 4

    def row(y):
        low, high, cross = (images_ref[pl.ds(k * pitch + y, 8, stride=pitch), :] for k in (0, 8, 4))
        plain, by_xi, by_eta = (jnp.broadcast_to(root_ref[k, pl.ds(y, 1), :], low.shape) for k in range(3))
        body = jnp.concatenate([low * plain, high * plain, low * by_xi, low * by_eta], axis=0)
        return body, jnp.where(upper, high, cross) * jnp.where(upper, by_xi, by_eta)

    def terms(start):
        body, rest = (jnp.concatenate(v, axis=1) for v in zip(*[row(start + j) for j in range(TURN)]))
        high, low = split(body)
        rest = jnp.concatenate([rest, rest - rest.astype(BF16).astype(F32)], axis=0).astype(BF16)
        short = jnp.concatenate([high, rest], axis=0)
        return short, jnp.concatenate([short, low], axis=0)

    first, second = first_ref[...], second_ref[...]
    step = size * len(starts) // 2
    near, far = starts[0], starts[0] + step if len(starts) == 1 else starts[1]
    for turn in range(0, step, TURN):
        short, whole = terms(near + turn)
        first = first + lax.dot_general(short, whole, NT, preferred_element_type=F32)
        short, whole = terms(far + turn)
        second = second + lax.dot_general(whole, short, NT, preferred_element_type=F32)
    first_ref[...], second_ref[...] = first, second


def combine(first_ref, second_ref):
    def pad(value, rows=SIDE):
        value = jnp.concatenate([value, jnp.zeros((value.shape[0], LANES - value.shape[1]), F32)], axis=1)
        if rows == value.shape[0]:
            return value
        return jnp.concatenate([value, jnp.zeros((rows - value.shape[0], LANES), F32)], axis=0)

    first, second = first_ref[:SIDE], second_ref[:, :SIDE]
    mixed = jnp.concatenate([first[:, DUAL:], first[:, SIDE:DUAL]], axis=1)
    mixed = mixed + jnp.concatenate([second[DUAL:], second[SIDE:DUAL]], axis=0)
    turned = jnp.transpose(pad(mixed, LANES))[:SIDE]
    return pad(first[:, :SIDE] + second[:SIDE]) + (pad(mixed) + turned)


def place(kind, b):
    if kind == 0:
        return b
    return (8 + 8 * kind + b) if b < 8 else (28 + 4 * kind + b - 8)


def solve(normal, count):
    side = SIDE
    row, col = iota((side, LANES), 0), iota((side, LANES), 1)
    unknowns = sorted([place(kind, b) for kind in range(3) for b in range(count)] + [count])

    def used(k):
        spare = [p for p in range(side) if p not in unknowns]
        keep = k < side
        for p in spare:
            keep = keep & (k != p)
        return keep

    rhs = normal[:, count + 1 : count + 2]
    system = jnp.where(used(row) & used(col), normal, 0.0) + ridge_weight * jnp.where(row == col, 1.0, 0.0)
    system = jnp.where((col == side) & used(row), rhs, system)
    scale = jnp.zeros((side, LANES), F32)
    for first in range(0, len(unknowns), BLOCK):
        block = unknowns[first : first + BLOCK]
        columns = [jnp.broadcast_to(system[:, p : p + 1], (side, LANES)) for p in block]
        for k, p in enumerate(block):
            column = columns[k]
            inverse = 1.0 / column[p : p + 1, :]
            scale = jnp.where(row == p, inverse, scale)
            factor = jnp.where(row == p, 0.0, column)
            for later in range(k + 1, len(block)):
                columns[later] = columns[later] - factor * (columns[later][p : p + 1, :] * inverse)
            system = system - factor * (system[p : p + 1, :] * inverse)
    return jnp.broadcast_to(system[:, side : side + 1], (side, LANES)) * scale


def apply(coefs, images_ref, science_ref, out_ref, pitch, count, total):
    _, rows, cols = science_ref.shape
    xi = xi_row(cols, total)
    wide = lambda k: jnp.broadcast_to(coefs[k : k + 1, :], (8, cols))
    flat = [wide(b) + wide(place(1, b)) * xi for b in range(count)]
    slope = [wide(place(2, b)) for b in range(count)]
    constant = wide(count)
    step = 8 if rows % 64 == 0 else 1

    def body(turn, carry):
        for k in range(step):
            start = pl.multiple_of((turn * step + k) * 8, 8)
            eta = 2.0 * (start + iota((8, cols), 0)).astype(F32) / rows - 1.0
            field = constant
            for b in range(count):
                field = field + images_ref[pl.ds(b * pitch + start, 8), :] * (flat[b] + slope[b] * eta)
            out_ref[0, pl.ds(start, 8), :] = science_ref[0, pl.ds(start, 8), :] - field
        return carry

    lax.fori_loop(0, rows // (8 * step), body, 0)


def remote(source, target, send, recv, epoch, tile):
    return pltpu.make_async_remote_copy(
        src_ref=source,
        dst_ref=target,
        send_sem=send,
        recv_sem=recv,
        device_id={"epoch": epoch, "tile": tile},
        device_id_type=pl.DeviceIdType.MESH,
    )


def kernel(total, top, pitch, template_in, science_in, rowp_in, colp_in, cov_in, srow_in, scol_in, out_ref,
           science_ref, rowp_ref, colp_ref, cov_ref, srow_ref, scol_ref,
           slots, pack, edges, across_ref, parts, mine, images_ref, root_ref, first_ref, second_ref, profile_ref,
           row_band_ref, col_band_ref, slot_send, slot_recv, edge_send, edge_recv,
           part_send, part_recv, load_sem, hello):
    count, taps = rowp_ref.shape
    _, rows, cols = science_ref.shape
    epochs, own_rows, _ = slots.shape
    tiles = parts.shape[0]
    size = row_band_ref.shape[1]
    epoch, tile = lax.axis_index("epoch"), lax.axis_index("tile")

    loads = [
        pltpu.make_async_copy(source, target, load_sem.at[k])
        for k, (source, target) in enumerate(
            [
                (template_in, slots.at[epoch]),
                (rowp_in, rowp_ref),
                (colp_in, colp_ref),
                (cov_in, cov_ref),
                (srow_in, srow_ref),
                (scol_in, scol_ref),
                (science_in, science_ref),
            ]
        )
    ]
    for load in loads:
        load.start()
    barrier = pltpu.get_barrier_semaphore()
    has_left, has_right = tile > 0, tile < tiles - 1

    def greet(semaphore, e, t):
        pl.semaphore_signal(semaphore, inc=1, device_id={"epoch": e, "tile": t}, device_id_type=pl.DeviceIdType.MESH)

    for t in range(1, tiles):
        greet(barrier, epoch, lax.rem(tile + t, tiles))

    def greet_above(target, carry):
        greet(barrier, target, tile)

        @pl.when(has_left)
        def _():
            greet(barrier, target, tile - 1)

        @pl.when(has_right)
        def _():
            greet(barrier, target, tile + 1)

        return carry

    lax.fori_loop(epoch + 1, epochs, greet_above, 0)
    loads[0].wait()
    flipped = jnp.transpose(slots[epoch])
    pack[0] = flipped[:EDGE]
    pack[1] = flipped[cols - EDGE :]
    around = 1 + has_left.astype(jnp.int32) + has_right.astype(jnp.int32)
    pl.semaphore_wait(barrier, tiles - 1 + epoch * around)

    def announce(target, carry):
        greet(hello.at[epoch], target, tile)
        return carry

    lax.fori_loop(0, epoch, announce, 0)

    def block_copy(target, source):
        return remote(slots.at[source], slots.at[source], slot_send.at[target], slot_recv.at[source], target, tile)

    def edge_copy(target, side, source):
        place = pl.ds((1 - side) * EDGE, EDGE)
        return remote(pack.at[side], edges.at[source, place], edge_send.at[side, target], edge_recv.at[1 - side, source],
                      target, tile + 2 * side - 1)

    def send(target, carry):
        @pl.when(target != epoch)
        def _():
            block_copy(target, epoch).start()

        for side, there in ((0, has_left), (1, has_right)):

            @pl.when(there)
            def _():
                edge_copy(target, side, epoch).start()

        return carry

    def send_up(target):
        @pl.when(target < epochs)
        def _():
            pl.semaphore_wait(hello.at[target], 1)
            send(target, 0)

    shift = jnp.where(epoch == epochs - 1, jnp.maximum(epochs - 2, 0), 0)
    lax.fori_loop(0, epoch + 1, lambda k, carry: send(lax.rem(k + shift, epoch + 1), carry), 0)

    for side, there in ((0, has_left), (1, has_right)):

        @pl.when(jnp.logical_not(there))
        def _():
            edges[:, side * EDGE : (side + 1) * EDGE, :] = jnp.zeros((epochs, EDGE, own_rows), F32)

    for load in loads[1:]:
        load.wait()
    make_bands(rowp_ref, colp_ref, profile_ref, row_band_ref, col_band_ref, top - taps // 2)
    high = across_ref.shape[1]
    across_ref[:, :top, :] = jnp.zeros((count, top, 2 * cols), BF16)
    across_ref[:, top + rows :, :] = jnp.zeros((count, high - top - rows, 2 * cols), BF16)

    make_weight(srow_ref, scol_ref, cov_ref, root_ref, total)
    images_ref[pl.ds(count * pitch, rows), :] = jnp.ones((rows, cols), F32)
    images_ref[pl.ds((count + 1) * pitch, rows), :] = science_ref[0]
    for spare in range(count + 2, GROUP):
        images_ref[pl.ds(spare * pitch, rows), :] = jnp.zeros((rows, cols), F32)
    send_up(epoch + 1)
    first_ref[...] = jnp.zeros_like(first_ref)
    second_ref[...] = jnp.zeros_like(second_ref)

    each = 2 * size // own_rows
    chunks = rows // (2 * size)
    middle = jnp.zeros((cols - 2 * EDGE, own_rows), F32)

    def columns(chunk):
        owns = [slots[chunk * each + k] for k in range(each)]
        sides = [jnp.transpose(jnp.concatenate([edges[chunk * each + k], middle], axis=0)) for k in range(each)]
        at = pl.ds(pl.multiple_of(top + chunk * 2 * size, 16), 2 * size)
        column_pass(jnp.concatenate(owns, axis=0), jnp.concatenate(sides, axis=0), at, col_band_ref, across_ref)

    def work(units):
        starts = [pl.multiple_of(unit * size, 16) for unit in units]
        row_pass(starts, row_band_ref, across_ref, images_ref, pitch)
        gram(starts, size, root_ref, images_ref, first_ref, second_ref, pitch)

    def arrive(source):
        @pl.when(source != epoch)
        def _():
            block_copy(epoch, source).wait_recv()

        for side, there in ((0, has_left), (1, has_right)):

            @pl.when(there)
            def _():
                edge_copy(epoch, 1 - side, source).wait_recv()

    def step(d, carry):
        @pl.when(d > 0)
        def _():
            send_up(epoch + d + 1)

        def side(k, carry):
            right = (k + (2 * epoch < epochs).astype(jnp.int32)) % 2 == 0
            source = epoch + jnp.where(right, d, -d)
            valid = (source >= 0) & (source < epochs) & ((d > 0) | (k == 0))

            @pl.when(valid)
            def _():
                arrive(source)

            if each == 1:

                @pl.when(valid)
                def _():
                    columns(source)

                @pl.when(valid & (d > 0))
                def _():
                    chunk = source + jnp.where(right, 0, 1)
                    work((2 * chunk - 1, 2 * chunk))

                def margin(turn, carry):
                    work((jnp.where((turn == 0) & (source == 0), 0, 2 * chunks - 1),))
                    return carry

                margins = (source == 0).astype(jnp.int32) + (source == epochs - 1).astype(jnp.int32)
                lax.fori_loop(0, jnp.where(valid, margins, 0), margin, 0)
            return carry

        lax.fori_loop(0, 2, side, 0)
        return carry

    lax.fori_loop(0, epochs, step, 0)
    if each > 1:

        def fresh_chunk(chunk, carry):
            columns(chunk)
            return carry

        def ready_chunk(chunk, carry):
            work((2 * chunk - 1, 2 * chunk))
            return carry

        def margin_unit(turn, carry):
            work((turn * (2 * chunks - 1),))
            return carry

        lax.fori_loop(0, chunks, fresh_chunk, 0)
        lax.fori_loop(1, chunks, ready_chunk, 0)
        lax.fori_loop(0, 2, margin_unit, 0)

    normal = combine(first_ref, second_ref)
    under = jnp.concatenate([normal[FOLD:], jnp.zeros((2 * FOLD - SIDE, LANES), F32)], axis=0)
    normal = normal[:FOLD] + shifted(under, HALF)
    mine[...] = normal

    def part_copy(t, source):
        return remote(mine, parts.at[source], part_send.at[t], part_recv.at[source],
                      epoch, lax.rem(tile + t, tiles))

    for t in sorted(range(1, tiles), key=lambda t: -t * (tiles - t)):
        part_copy(t, tile).start()
    for t in range(1, tiles):
        source = lax.rem(tile + tiles - t, tiles)
        part_copy(t, source).wait_recv()
        normal = normal + parts[source]


    lane = iota((1, LANES), 1)
    normal = jnp.concatenate(
        [jnp.where(lane < HALF, normal, 0.0), jnp.where(lane < HALF, shifted(normal, HALF), 0.0)[: SIDE - FOLD]], axis=0
    )
    coefs = solve(normal, count)
    apply(coefs, images_ref, science_ref, out_ref, pitch, count, total)

    for t in range(1, tiles):
        part_copy(t, tile).wait_send()

    def sent(target, carry):
        @pl.when(target != epoch)
        def _():
            block_copy(target, epoch).wait_send()

        for side, there in ((0, has_left), (1, has_right)):

            @pl.when(there)
            def _():
                edge_copy(target, side, epoch).wait_send()

        return carry

    lax.fori_loop(0, epochs, sent, 0)


def local(template, science, row_profiles, col_profiles, coverage, stamp_rows, stamp_cols):
    count, taps = row_profiles.shape
    rows, cols = science.shape[1:]
    own_rows = template.shape[0]
    tiles, epochs = lax.axis_size("tile"), lax.axis_size("epoch")
    top = -(-(taps // 2) // 16) * 16
    size = unit_rows(rows, own_rows, top)
    pitch = rows + 4
    vmem = pl.BlockSpec(memory_space=pltpu.VMEM)
    dma = pltpu.SemaphoreType.DMA
    operands = (
        template,
        science,
        row_profiles,
        col_profiles,
        coverage,
        stamp_rows.reshape(1, -1),
        stamp_cols.reshape(1, -1),
    )
    return pl.pallas_call(
        functools.partial(kernel, cols * tiles, top, pitch),
        out_shape=jax.ShapeDtypeStruct(science.shape, F32),
        in_specs=[pl.BlockSpec(memory_space=pl.ANY)] * 7,
        out_specs=vmem,
        scratch_shapes=[
            pltpu.VMEM(science.shape, F32),
            pltpu.VMEM(row_profiles.shape, F32),
            pltpu.VMEM(col_profiles.shape, F32),
            pltpu.VMEM(coverage.shape, jnp.int32),
            pltpu.VMEM((1, stamp_rows.shape[0]), jnp.int32),
            pltpu.VMEM((1, stamp_cols.shape[0]), jnp.int32),
            pltpu.VMEM((epochs, own_rows, cols), F32),
            pltpu.VMEM((2, EDGE, own_rows), F32),
            pltpu.VMEM((epochs, 2 * EDGE, own_rows), F32),
            pltpu.VMEM((count, rows + 2 * top, 2 * cols), BF16),
            pltpu.VMEM((tiles, FOLD, LANES), F32),
            pltpu.VMEM((FOLD, LANES), F32),
            pltpu.VMEM((GROUP * pitch, cols), F32),
            pltpu.VMEM((3, rows, cols), F32),
            pltpu.VMEM((DUAL, BOTH), F32),
            pltpu.VMEM((BOTH, DUAL), F32),
            pltpu.VMEM((3, GROUP, 2 * LANES), F32),
            pltpu.VMEM((count, size, 3 * (size + 2 * top)), BF16),
            pltpu.VMEM((-(-count // 2), 4 * LANES, 2 * LANES), BF16),
            dma((epochs,)),
            dma((epochs,)),
            dma((2, epochs)),
            dma((2, epochs)),
            dma((tiles,)),
            dma((tiles,)),
            dma((7,)),
            pltpu.SemaphoreType.REGULAR((epochs,)),
        ],
        compiler_params=pltpu.CompilerParams(
            collective_id=0, has_side_effects=True, vmem_limit_bytes=48 * 2**20
        ),
    )(*(pltpu.with_memory_space_constraint(operand, pltpu.HBM) for operand in operands))


def solution(mesh):
    in_specs = (
        P(("patch", "epoch"), "tile"),
        P(("patch", "epoch"), None, "tile"),
        P(),
        P(),
        P(("patch", "epoch"), "tile"),
        P(("patch", "tile")),
        P(("patch", "tile")),
    )
    out_specs = P(("patch", "epoch"), None, "tile")
    return jax.shard_map(local, mesh=mesh, in_specs=in_specs, out_specs=out_specs, check_vma=False)
```

```python
import functools

import jax
import jax.numpy as jnp
from jax import lax
from jax.experimental import pallas as pl
from jax.experimental.pallas import tpu as pltpu
from jax.sharding import PartitionSpec as P

S = 32
GROUP = 16
EDGE = 16
LANES = 128
HALF = LANES // 2
BLOCK = 13
SIDE = 40
TURN = 8
FOLD = 24
DUAL = 48
BOTH = 80
ridge_weight = 1.0
F32 = jnp.float32
BF16 = jnp.bfloat16
NT = (((1,), (1,)), ((), ()))
NN = (((1,), (0,)), ((), ()))


def split(value):
    high = value.astype(BF16)
    return high, (value - high.astype(F32)).astype(BF16)


def iota(shape, axis):
    return lax.broadcasted_iota(jnp.int32, shape, axis)


def shifted(value, turn):
    turn %= value.shape[1]
    return pltpu.roll(value, turn, 1) if turn else value


def toeplitz(profile_row, rows, turn=0):
    width = profile_row.shape[1]
    base = pltpu.roll(jnp.broadcast_to(profile_row, (8, width)), 0, 1, stride=1, stride_axis=0)
    return jnp.concatenate([shifted(base, turn + first) for first in range(0, rows, 8)], axis=0)


def xi_row(cols, total):
    start = lax.axis_index("tile") * cols
    return 2.0 * (start + iota((1, cols), 1)).astype(F32) / total - 1.0


def unit_rows(rows, own, top):
    sizes = [r for r in range(16, 2 * LANES // 3 - 2 * top + 1, 16) if rows % (2 * r) == 0 and 2 * r % own == 0]
    return max(sizes)


def make_bands(rowp_ref, colp_ref, profile_ref, row_band_ref, col_band_ref, shift):
    count, taps = rowp_ref.shape
    half = taps // 2
    profile_ref[...] = jnp.zeros_like(profile_ref)
    high, low = (part.astype(F32) for part in split(rowp_ref[...]))
    _, size, width = row_band_ref.shape
    for k, part in enumerate((high, high, low)):
        at = k * (width // 3) + shift
        profile_ref[0, :count, at : at + taps] = part
    flip = jnp.where(iota((taps, taps), 0) + iota((taps, taps), 1) == taps - 1, 1.0, 0.0).astype(BF16)
    for k, part in enumerate(split(colp_ref[...])):
        profile_ref[1 + k, :count, :taps] = lax.dot_general(part, flip, NN, preferred_element_type=F32)
    gap = jnp.zeros((LANES - 6 * EDGE, LANES), BF16)
    for b in range(count):
        row_band_ref[b] = toeplitz(profile_ref[0, b : b + 1, :], size)[:, :width].astype(BF16)
        parts = []
        for k in (1, 2):
            tall = toeplitz(profile_ref[k, b : b + 1, :], LANES + 2 * EDGE, -half - EDGE)[:, :LANES].astype(BF16)
            beside = jnp.concatenate([tall[:EDGE], tall[EDGE + LANES :]], axis=0)
            parts.append((tall[EDGE : EDGE + LANES], beside))
        (high, near_high), (low, near_low) = parts
        at = pl.ds((b % 2) * LANES, LANES)
        column = jnp.concatenate([high, high, low, near_high, near_high, near_low, gap], axis=0)
        col_band_ref[b // 2, :, at] = column


def column_pass(own, beside, at, col_band_ref, across_ref):
    count = across_ref.shape[0]
    lane = iota((1, LANES), 1)
    high, low = split(own)
    near = jnp.where(lane < 2 * EDGE, beside, 0.0)
    near_high = near.astype(BF16).astype(F32)
    near_low = near - near_high
    near = near_high + shifted(near_low, 2 * EDGE) + shifted(near_high, 4 * EDGE)
    terms = jnp.concatenate([high, low, high, near.astype(BF16)], axis=1)
    for pair in range(0, count, 2):
        both = lax.dot_general(terms, col_band_ref[pair // 2], NN, preferred_element_type=F32)
        for k, b in enumerate(range(pair, min(pair + 2, count))):
            across_ref[b, at, :] = jnp.concatenate(split(both[:, k * LANES : (k + 1) * LANES]), axis=1)


def row_pass(starts, row_band_ref, across_ref, images_ref, pitch):
    count = across_ref.shape[0]
    _, size, width = row_band_ref.shape
    for b in range(count):
        sides = []
        for start in starts:
            across = across_ref[b, pl.ds(start, width // 3), :]
            sides.append(jnp.concatenate([across[:, :LANES], across[:, LANES:], across[:, :LANES]], axis=0))
        both = lax.dot_general(
            row_band_ref[b], jnp.concatenate(sides, axis=1), NN, preferred_element_type=F32
        )
        for k, start in enumerate(starts):
            images_ref[pl.ds(b * pitch + start, size), :] = both[:, k * LANES : (k + 1) * LANES]


def make_weight(srow_ref, scol_ref, cov_ref, root_ref, total):
    _, rows, cols = root_ref.shape
    stamps = srow_ref.shape[1]
    at = iota((cols, stamps), 0) - scol_ref[...]
    cols_in = jnp.where((at >= 0) & (at < S), cov_ref[...].astype(F32), 0.0).astype(BF16)
    at = iota((rows, stamps), 0) - srow_ref[...]
    rows_in = jnp.where((at >= 0) & (at < S), 1.0, 0.0).astype(BF16)
    root = jnp.sqrt(lax.dot_general(rows_in, cols_in, NT, preferred_element_type=F32))
    root_ref[0] = root
    root_ref[1] = root * xi_row(cols, total)
    root_ref[2] = root * (2.0 * iota((rows, 1), 0).astype(F32) / rows - 1.0)


def gram(starts, size, root_ref, images_ref, first_ref, second_ref, pitch):
    upper = iota((8, images_ref.shape[1]), 0) < 4

    def row(y):
        low, high, cross = (images_ref[pl.ds(k * pitch + y, 8, stride=pitch), :] for k in (0, 8, 4))
        plain, by_xi, by_eta = (jnp.broadcast_to(root_ref[k, pl.ds(y, 1), :], low.shape) for k in range(3))
        body = jnp.concatenate([low * plain, high * plain, low * by_xi, low * by_eta], axis=0)
        return body, jnp.where(upper, high, cross) * jnp.where(upper, by_xi, by_eta)

    def terms(start):
        body, rest = (jnp.concatenate(v, axis=1) for v in zip(*[row(start + j) for j in range(TURN)]))
        high, low = split(body)
        rest = jnp.concatenate([rest, rest - rest.astype(BF16).astype(F32)], axis=0).astype(BF16)
        short = jnp.concatenate([high, rest], axis=0)
        return short, jnp.concatenate([short, low], axis=0)

    first, second = first_ref[...], second_ref[...]
    step = size * len(starts) // 2
    near, far = starts[0], starts[0] + step if len(starts) == 1 else starts[1]
    for turn in range(0, step, TURN):
        short, whole = terms(near + turn)
        first = first + lax.dot_general(short, whole, NT, preferred_element_type=F32)
        short, whole = terms(far + turn)
        second = second + lax.dot_general(whole, short, NT, preferred_element_type=F32)
    first_ref[...], second_ref[...] = first, second


def combine(first_ref, second_ref):
    def pad(value, rows=SIDE):
        value = jnp.concatenate([value, jnp.zeros((value.shape[0], LANES - value.shape[1]), F32)], axis=1)
        if rows == value.shape[0]:
            return value
        return jnp.concatenate([value, jnp.zeros((rows - value.shape[0], LANES), F32)], axis=0)

    first, second = first_ref[:SIDE], second_ref[:, :SIDE]
    mixed = jnp.concatenate([first[:, DUAL:], first[:, SIDE:DUAL]], axis=1)
    mixed = mixed + jnp.concatenate([second[DUAL:], second[SIDE:DUAL]], axis=0)
    turned = jnp.transpose(pad(mixed, LANES))[:SIDE]
    return pad(first[:, :SIDE] + second[:SIDE]) + (pad(mixed) + turned)


def place(kind, b):
    if kind == 0:
        return b
    return (8 + 8 * kind + b) if b < 8 else (28 + 4 * kind + b - 8)


def solve(normal, count):
    side = SIDE
    row, col = iota((side, LANES), 0), iota((side, LANES), 1)
    unknowns = sorted([place(kind, b) for kind in range(3) for b in range(count)] + [count])

    def used(k):
        spare = [p for p in range(side) if p not in unknowns]
        keep = k < side
        for p in spare:
            keep = keep & (k != p)
        return keep

    rhs = normal[:, count + 1 : count + 2]
    system = jnp.where(used(row) & used(col), normal, 0.0) + ridge_weight * jnp.where(row == col, 1.0, 0.0)
    system = jnp.where((col == side) & used(row), rhs, system)
    scale = jnp.zeros((side, LANES), F32)
    for first in range(0, len(unknowns), BLOCK):
        block = unknowns[first : first + BLOCK]
        columns = [jnp.broadcast_to(system[:, p : p + 1], (side, LANES)) for p in block]
        for k, p in enumerate(block):
            column = columns[k]
            inverse = 1.0 / column[p : p + 1, :]
            scale = jnp.where(row == p, inverse, scale)
            factor = jnp.where(row == p, 0.0, column)
            for later in range(k + 1, len(block)):
                columns[later] = columns[later] - factor * (columns[later][p : p + 1, :] * inverse)
            system = system - factor * (system[p : p + 1, :] * inverse)
    return jnp.broadcast_to(system[:, side : side + 1], (side, LANES)) * scale


def apply(coefs, images_ref, science_ref, out_ref, pitch, count, total):
    _, rows, cols = science_ref.shape
    xi = xi_row(cols, total)
    wide = lambda k: jnp.broadcast_to(coefs[k : k + 1, :], (8, cols))
    flat = [wide(b) + wide(place(1, b)) * xi for b in range(count)]
    slope = [wide(place(2, b)) for b in range(count)]
    constant = wide(count)
    step = 8 if rows % 64 == 0 else 1

    def body(turn, carry):
        for k in range(step):
            start = pl.multiple_of((turn * step + k) * 8, 8)
            eta = 2.0 * (start + iota((8, cols), 0)).astype(F32) / rows - 1.0
            field = constant
            for b in range(count):
                field = field + images_ref[pl.ds(b * pitch + start, 8), :] * (flat[b] + slope[b] * eta)
            out_ref[0, pl.ds(start, 8), :] = science_ref[0, pl.ds(start, 8), :] - field
        return carry

    lax.fori_loop(0, rows // (8 * step), body, 0)


def remote(source, target, send, recv, epoch, tile):
    return pltpu.make_async_remote_copy(
        src_ref=source,
        dst_ref=target,
        send_sem=send,
        recv_sem=recv,
        device_id={"epoch": epoch, "tile": tile},
        device_id_type=pl.DeviceIdType.MESH,
    )


def kernel(total, top, pitch, template_in, science_in, rowp_in, colp_in, cov_in, srow_in, scol_in, out_ref,
           science_ref, rowp_ref, colp_ref, cov_ref, srow_ref, scol_ref,
           slots, pack, edges, across_ref, parts, mine, images_ref, root_ref, first_ref, second_ref, profile_ref,
           row_band_ref, col_band_ref, slot_send, slot_recv, edge_send, edge_recv,
           part_send, part_recv, load_sem, hello):
    count, taps = rowp_ref.shape
    _, rows, cols = science_ref.shape
    epochs, own_rows, _ = slots.shape
    tiles = parts.shape[0]
    size = row_band_ref.shape[1]
    epoch, tile = lax.axis_index("epoch"), lax.axis_index("tile")

    loads = [
        pltpu.make_async_copy(source, target, load_sem.at[k])
        for k, (source, target) in enumerate(
            [
                (template_in, slots.at[epoch]),
                (rowp_in, rowp_ref),
                (colp_in, colp_ref),
                (cov_in, cov_ref),
                (srow_in, srow_ref),
                (scol_in, scol_ref),
                (science_in, science_ref),
            ]
        )
    ]
    for load in loads:
        load.start()
    barrier = pltpu.get_barrier_semaphore()
    has_left, has_right = tile > 0, tile < tiles - 1

    def greet(semaphore, e, t):
        pl.semaphore_signal(semaphore, inc=1, device_id={"epoch": e, "tile": t}, device_id_type=pl.DeviceIdType.MESH)

    for t in range(1, tiles):
        greet(barrier, epoch, lax.rem(tile + t, tiles))

    def greet_above(target, carry):
        greet(barrier, target, tile)

        @pl.when(has_left)
        def _():
            greet(barrier, target, tile - 1)

        @pl.when(has_right)
        def _():
            greet(barrier, target, tile + 1)

        return carry

    lax.fori_loop(epoch + 1, epochs, greet_above, 0)
    loads[0].wait()
    flipped = jnp.transpose(slots[epoch])
    pack[0] = flipped[:EDGE]
    pack[1] = flipped[cols - EDGE :]
    around = 1 + has_left.astype(jnp.int32) + has_right.astype(jnp.int32)
    pl.semaphore_wait(barrier, tiles - 1 + epoch * around)

    def announce(target, carry):
        greet(hello.at[epoch], target, tile)
        return carry

    lax.fori_loop(0, epoch, announce, 0)

    def block_copy(target, source):
        return remote(slots.at[source], slots.at[source], slot_send.at[target], slot_recv.at[source], target, tile)

    def edge_copy(target, side, source):
        place = pl.ds((1 - side) * EDGE, EDGE)
        return remote(pack.at[side], edges.at[source, place], edge_send.at[side, target], edge_recv.at[1 - side, source],
                      target, tile + 2 * side - 1)

    def send(target, carry):
        @pl.when(target != epoch)
        def _():
            block_copy(target, epoch).start()

        for side, there in ((0, has_left), (1, has_right)):

            @pl.when(there)
            def _():
                edge_copy(target, side, epoch).start()

        return carry

    def send_up(target):
        @pl.when(target < epochs)
        def _():
            pl.semaphore_wait(hello.at[target], 1)
            send(target, 0)

    shift = jnp.where(epoch == epochs - 1, jnp.maximum(epochs - 2, 0), 0)
    lax.fori_loop(0, epoch + 1, lambda k, carry: send(lax.rem(k + shift, epoch + 1), carry), 0)

    for side, there in ((0, has_left), (1, has_right)):

        @pl.when(jnp.logical_not(there))
        def _():
            edges[:, side * EDGE : (side + 1) * EDGE, :] = jnp.zeros((epochs, EDGE, own_rows), F32)

    for load in loads[1:]:
        load.wait()
    make_bands(rowp_ref, colp_ref, profile_ref, row_band_ref, col_band_ref, top - taps // 2)
    high = across_ref.shape[1]
    across_ref[:, :top, :] = jnp.zeros((count, top, 2 * cols), BF16)
    across_ref[:, top + rows :, :] = jnp.zeros((count, high - top - rows, 2 * cols), BF16)

    make_weight(srow_ref, scol_ref, cov_ref, root_ref, total)
    images_ref[pl.ds(count * pitch, rows), :] = jnp.ones((rows, cols), F32)
    images_ref[pl.ds((count + 1) * pitch, rows), :] = science_ref[0]
    for spare in range(count + 2, GROUP):
        images_ref[pl.ds(spare * pitch, rows), :] = jnp.zeros((rows, cols), F32)
    send_up(epoch + 1)
    first_ref[...] = jnp.zeros_like(first_ref)
    second_ref[...] = jnp.zeros_like(second_ref)

    each = 2 * size // own_rows
    chunks = rows // (2 * size)
    middle = jnp.zeros((cols - 2 * EDGE, own_rows), F32)

    def columns(chunk):
        owns = [slots[chunk * each + k] for k in range(each)]
        sides = [jnp.transpose(jnp.concatenate([edges[chunk * each + k], middle], axis=0)) for k in range(each)]
        at = pl.ds(pl.multiple_of(top + chunk * 2 * size, 16), 2 * size)
        column_pass(jnp.concatenate(owns, axis=0), jnp.concatenate(sides, axis=0), at, col_band_ref, across_ref)

    def work(units):
        starts = [pl.multiple_of(unit * size, 16) for unit in units]
        row_pass(starts, row_band_ref, across_ref, images_ref, pitch)
        gram(starts, size, root_ref, images_ref, first_ref, second_ref, pitch)

    def arrive(source):
        @pl.when(source != epoch)
        def _():
            block_copy(epoch, source).wait_recv()

        for side, there in ((0, has_left), (1, has_right)):

            @pl.when(there)
            def _():
                edge_copy(epoch, 1 - side, source).wait_recv()

    def step(d, carry):
        @pl.when(d > 0)
        def _():
            send_up(epoch + d + 1)

        def side(k, carry):
            right = (k + (2 * epoch < epochs).astype(jnp.int32)) % 2 == 0
            source = epoch + jnp.where(right, d, -d)
            valid = (source >= 0) & (source < epochs) & ((d > 0) | (k == 0))

            @pl.when(valid)
            def _():
                arrive(source)

            if each == 1:

                @pl.when(valid & (d == 0))
                def _():
                    columns(source)

                @pl.when(valid & (d > 0))
                def _():
                    columns(source)
                    chunk = source + jnp.where(right, 0, 1)
                    work((2 * chunk - 1, 2 * chunk))

                def margin(turn, carry):
                    work((jnp.where((turn == 0) & (source == 0), 0, 2 * chunks - 1),))
                    return carry

                margins = (source == 0).astype(jnp.int32) + (source == epochs - 1).astype(jnp.int32)
                lax.fori_loop(0, jnp.where(valid, margins, 0), margin, 0)
            return carry

        lax.fori_loop(0, 2, side, 0)
        return carry

    lax.fori_loop(0, epochs, step, 0)
    if each > 1:

        def fresh_chunk(chunk, carry):
            columns(chunk)
            return carry

        def ready_chunk(chunk, carry):
            work((2 * chunk - 1, 2 * chunk))
            return carry

        def margin_unit(turn, carry):
            work((turn * (2 * chunks - 1),))
            return carry

        lax.fori_loop(0, chunks, fresh_chunk, 0)
        lax.fori_loop(1, chunks, ready_chunk, 0)
        lax.fori_loop(0, 2, margin_unit, 0)

    normal = combine(first_ref, second_ref)
    under = jnp.concatenate([normal[FOLD:], jnp.zeros((2 * FOLD - SIDE, LANES), F32)], axis=0)
    normal = normal[:FOLD] + shifted(under, HALF)
    mine[...] = normal

    def part_copy(t, source):
        return remote(mine, parts.at[source], part_send.at[t], part_recv.at[source],
                      epoch, lax.rem(tile + t, tiles))

    for t in sorted(range(1, tiles), key=lambda t: -t * (tiles - t)):
        part_copy(t, tile).start()
    for t in range(1, tiles):
        source = lax.rem(tile + tiles - t, tiles)
        part_copy(t, source).wait_recv()
        normal = normal + parts[source]


    lane = iota((1, LANES), 1)
    normal = jnp.concatenate(
        [jnp.where(lane < HALF, normal, 0.0), jnp.where(lane < HALF, shifted(normal, HALF), 0.0)[: SIDE - FOLD]], axis=0
    )
    coefs = solve(normal, count)
    apply(coefs, images_ref, science_ref, out_ref, pitch, count, total)

    for t in range(1, tiles):
        part_copy(t, tile).wait_send()

    def sent(target, carry):
        @pl.when(target != epoch)
        def _():
            block_copy(target, epoch).wait_send()

        for side, there in ((0, has_left), (1, has_right)):

            @pl.when(there)
            def _():
                edge_copy(target, side, epoch).wait_send()

        return carry

    lax.fori_loop(0, epochs, sent, 0)


def local(template, science, row_profiles, col_profiles, coverage, stamp_rows, stamp_cols):
    count, taps = row_profiles.shape
    rows, cols = science.shape[1:]
    own_rows = template.shape[0]
    tiles, epochs = lax.axis_size("tile"), lax.axis_size("epoch")
    top = -(-(taps // 2) // 16) * 16
    size = unit_rows(rows, own_rows, top)
    pitch = rows + 4
    vmem = pl.BlockSpec(memory_space=pltpu.VMEM)
    dma = pltpu.SemaphoreType.DMA
    operands = (
        template,
        science,
        row_profiles,
        col_profiles,
        coverage,
        stamp_rows.reshape(1, -1),
        stamp_cols.reshape(1, -1),
    )
    return pl.pallas_call(
        functools.partial(kernel, cols * tiles, top, pitch),
        out_shape=jax.ShapeDtypeStruct(science.shape, F32),
        in_specs=[pl.BlockSpec(memory_space=pl.ANY)] * 7,
        out_specs=vmem,
        scratch_shapes=[
            pltpu.VMEM(science.shape, F32),
            pltpu.VMEM(row_profiles.shape, F32),
            pltpu.VMEM(col_profiles.shape, F32),
            pltpu.VMEM(coverage.shape, jnp.int32),
            pltpu.VMEM((1, stamp_rows.shape[0]), jnp.int32),
            pltpu.VMEM((1, stamp_cols.shape[0]), jnp.int32),
            pltpu.VMEM((epochs, own_rows, cols), F32),
            pltpu.VMEM((2, EDGE, own_rows), F32),
            pltpu.VMEM((epochs, 2 * EDGE, own_rows), F32),
            pltpu.VMEM((count, rows + 2 * top, 2 * cols), BF16),
            pltpu.VMEM((tiles, FOLD, LANES), F32),
            pltpu.VMEM((FOLD, LANES), F32),
            pltpu.VMEM((GROUP * pitch, cols), F32),
            pltpu.VMEM((3, rows, cols), F32),
            pltpu.VMEM((DUAL, BOTH), F32),
            pltpu.VMEM((BOTH, DUAL), F32),
            pltpu.VMEM((3, GROUP, 2 * LANES), F32),
            pltpu.VMEM((count, size, 3 * (size + 2 * top)), BF16),
            pltpu.VMEM((-(-count // 2), 4 * LANES, 2 * LANES), BF16),
            dma((epochs,)),
            dma((epochs,)),
            dma((2, epochs)),
            dma((2, epochs)),
            dma((tiles,)),
            dma((tiles,)),
            dma((7,)),
            pltpu.SemaphoreType.REGULAR((epochs,)),
        ],
        compiler_params=pltpu.CompilerParams(
            collective_id=0, has_side_effects=True, vmem_limit_bytes=48 * 2**20
        ),
    )(*(pltpu.with_memory_space_constraint(operand, pltpu.HBM) for operand in operands))


def solution(mesh):
    in_specs = (
        P(("patch", "epoch"), "tile"),
        P(("patch", "epoch"), None, "tile"),
        P(),
        P(),
        P(("patch", "epoch"), "tile"),
        P(("patch", "tile")),
        P(("patch", "tile")),
    )
    out_specs = P(("patch", "epoch"), None, "tile")
    return jax.shard_map(local, mesh=mesh, in_specs=in_specs, out_specs=out_specs, check_vma=False)
```
